512 devices in a mesh: dp: 32 (over x, z), tp: 16 (over y, core).
Axes of the slice: x: 4, y: 8, z: 8, core: 2. Of those that a mesh axis runs over, the one named last changes fastest.
Arguments:
- queries: bfloat16 [1024, 128, 576], P(('dp', 'tp')), may hold values from -40 to 40
- latent_cache: bfloat16 [1024, 256, 576], P(('dp', 'tp')), may hold values from -5 to 5
- lengths: int32 [1024], P(('dp', 'tp')), may hold values from 1 to 256, 65536 in all
- value_weight: bfloat16 [128, 512, 128], P('tp'), may hold values from -0.25 to 0.25
- output_weight: bfloat16 [16384, 7168], P('tp', 'dp'), may hold values from -0.046875 to 0.046875
Outputs:
- attended: bfloat16 [1024, 7168], P(('dp', 'tp'))
The draws below stay inside these ranges and needn't reach their ends.
All inputs are finite; a program needn't handle non-finite values. No bound on the sum of `lengths` on one device may be relied on, other than what follows from the above.
Results may differ from the reference program's by a relative error of at most 0.0065.
Values may be sent and summed in bfloat16 or wider, within the bound.
No kernel may reach another device: no remote copies, remote signals or barrier semaphores. Data moves between devices by JAX's collectives and lax.ppermute only.
A program may use at most 64 MiB of HBM per device.

```python
import math
import jax
import jax.numpy as jnp
import numpy as np
from jax import lax

H = 128
DL = 512
DR = 64
DV = 128
D = 7168
REQ_DEV = 2
LMAX = 256
REQS = 1024


def clipped_normal(key, shape):
    return jnp.clip(jax.random.normal(key, shape, jnp.float32), -4.0, 4.0)


def first_slots(key):
    return clipped_normal(jax.random.fold_in(key, 105), (REQS, DL + DR))


def draw_latent_cache(key, part):
    base = clipped_normal(jax.random.fold_in(key, 101), (REQS, LMAX, DL + DR))
    base = base.at[:, 0, :].set(first_slots(key))
    return base.astype(jnp.bfloat16)


def draw_queries(key, part):
    base = clipped_normal(jax.random.fold_in(key, 104), (REQS, H, DL + DR))
    return base.astype(jnp.bfloat16)


def levels(key, extent, split, low, top_value):
    def one(position, shards_of):
        draws = jax.random.uniform(jax.random.fold_in(jax.random.fold_in(key, 6), position), (shards_of,), jnp.float32, low / len(split), top_value / len(split))
        return jnp.repeat(jnp.exp(draws), extent[position] // shards_of).reshape((-1,) + (1,) * (len(extent) - position - 1))

    level = one(*split[0])
    for cut in split[1:]:
        level = level * one(*cut)
    return level


def split_up(amount, total, limit, lean):
    portions = [(1 << 20) // math.isqrt(grade ** lean) + 1 for grade in range(2, amount + 1)]
    surplus, counts = total - limit - (amount - 1), [1] * (amount - 1)
    while surplus > 0:
        free = [i for i in range(amount - 1) if counts[i] < limit]
        pool, remaining = sum([portions[i] for i in free]), surplus
        for i in free:
            more = min(limit - counts[i], max(1, remaining * portions[i] // pool), surplus)
            counts[i] = counts[i] + more
            surplus = surplus - more
    return np.array([limit] + counts)


def uneven_parts(rng, amount, total, reach, skew):
    if amount == 2:
        one = jax.random.randint(rng, (), max(1, total - reach), min(reach, total - 1) + 1)
        return jnp.stack([one, total - one])
    tallies = jnp.asarray(split_up(amount, total, reach, skew), jnp.int32)
    couples = (amount - 1) // 2
    giver, taker = tallies[1:1 + 2 * couples:2], tallies[2:2 + 2 * couples:2]
    slack = jnp.minimum(giver - 1, reach - taker)
    moved = jax.random.randint(jax.random.fold_in(rng, 1), (couples,), 0, 1 << 20) % (slack + 1)
    tallies = tallies.at[1:1 + 2 * couples:2].set(giver - moved).at[2:2 + 2 * couples:2].set(taker + moved)
    return tallies[jax.random.permutation(jax.random.fold_in(rng, 2), amount)]


def normal_values(rng, dims, spread, limit, pieces=(), kind=jnp.bfloat16):
    entries = jax.random.normal(rng, dims, jnp.float32) * spread
    if len(pieces) > 0:
        entries = levels(rng, dims, pieces, -0.22, 0.18) * entries
    return jnp.clip(entries, min=-limit, max=limit).astype(kind)


def setup_inputs(seed: int = 0) -> dict:
    streams_of = jax.random.split(jax.random.key(seed), 6)
    queries = draw_queries(jax.random.fold_in(streams_of[5], 71), 0)
    latent_cache = draw_latent_cache(jax.random.fold_in(streams_of[5], 71), 0)
    lengths = uneven_parts(streams_of[2], REQS, REQS * LMAX // 4, LMAX, 2).astype(jnp.int32)
    value_weight = normal_values(streams_of[3], (H, DL, DV), DL ** -0.5, 0.25, ((0, 16),))
    output_weight = normal_values(streams_of[4], (H * DV, D), (H * DV) ** -0.5, 0.046875, ((0, 16), (1, 32)))
    return dict(queries=queries, latent_cache=latent_cache, lengths=lengths, value_weight=value_weight, output_weight=output_weight)


score_scale = 192.0 ** -0.5


def attend_block(queries, latent_cache, lengths, value_weight):
    scores = jnp.einsum("rhe,rje->rhj", queries.astype(jnp.float32), latent_cache.astype(jnp.float32)) * score_scale
    alive = jnp.arange(latent_cache.shape[1], dtype=jnp.int32)[None, None, :] < lengths[:, None, None]
    scores = jnp.where(alive, scores, -1e30)
    row_max = jnp.max(scores, axis=2, keepdims=True)
    powers = jnp.exp(scores - row_max)
    weights = (powers / jnp.sum(powers, axis=2, keepdims=True)).astype(jnp.bfloat16)
    mixture = jnp.einsum("rhj,rje->rhe", weights.astype(jnp.float32), latent_cache.astype(jnp.float32))
    latent = mixture[:, :, :DL].astype(jnp.bfloat16)
    values = jnp.einsum("rhd,hde->rhe", latent.astype(jnp.float32), value_weight.astype(jnp.float32))
    return values.astype(jnp.bfloat16)


def reference(queries, latent_cache, lengths, value_weight, output_weight):
    block_count = REQS // REQ_DEV
    stacked_queries = queries.reshape(block_count, REQ_DEV, H, DL + DR)
    stacked_cache = latent_cache.reshape(block_count, REQ_DEV, LMAX, DL + DR)
    stacked_lengths = lengths.reshape(block_count, REQ_DEV)

    def one_block(item):
        return attend_block(item[0], item[1], item[2], value_weight)

    values = lax.map(one_block, (stacked_queries, stacked_cache, stacked_lengths))
    values = values.reshape(REQS, H * DV)
    return jnp.dot(values, output_weight, preferred_element_type=jnp.float32).astype(jnp.bfloat16)
```

```python
import jax
import jax.numpy as jnp
from jax import lax
from jax.sharding import PartitionSpec as P

score_scale = 192.0 ** (-0.5)


def local(queries, latent_cache, lengths, value_weight, output_weight):
    requests = queries.shape[0]
    groups = lax.axis_size("tp")
    columns = lax.axis_size("dp")
    latent_width = value_weight.shape[1]
    scores = (
        jnp.einsum("rhe,rje->rhj", queries, latent_cache, preferred_element_type=jnp.float32)
        * score_scale
    )
    alive_mask = lax.broadcasted_iota(jnp.int32, scores.shape, 2) < lengths[:, None, None]
    scores = jnp.where(alive_mask, scores, -1e30)
    row_max = jnp.max(scores, axis=2, keepdims=True)
    powers = jnp.exp(scores - row_max)
    weights = (powers / jnp.sum(powers, axis=2, keepdims=True)).astype(jnp.bfloat16)
    mixture = jnp.einsum("rhj,rje->rhe", weights, latent_cache, preferred_element_type=jnp.float32)
    latent = mixture[:, :, :latent_width].astype(jnp.bfloat16)
    swapped = lax.all_to_all(latent, "tp", split_axis=1, concat_axis=0, tiled=True)
    values = jnp.einsum("qhd,hde->qhe", swapped, value_weight, preferred_element_type=jnp.float32)
    values = values.astype(jnp.bfloat16).reshape(groups, requests, -1)
    everyone = lax.all_gather(values, "dp", axis=1, tiled=True)
    all_values = everyone.reshape(groups * columns * requests, -1)
    summed = lax.psum_scatter(
        jnp.dot(all_values, output_weight, preferred_element_type=jnp.float32),
        "tp",
        scatter_dimension=0,
        tiled=True,
    )
    rounded = summed.astype(jnp.bfloat16)
    return lax.all_to_all(rounded, "dp", split_axis=0, concat_axis=1, tiled=True)


def solution(mesh):
    return jax.shard_map(
        local,
        mesh=mesh,
        in_specs=(
            P(("dp", "tp"), None, None),
            P(("dp", "tp"), None, None),
            P(("dp", "tp")),
            P("tp", None, None),
            P("tp", "dp"),
        ),
        out_specs=P(("dp", "tp"), None),
        check_vma=False,
    )
```

```python
import jax
import jax.numpy as jnp
from jax import lax
from jax.sharding import Mesh
from jax.sharding import PartitionSpec as P

score_scale = 192.0 ** (-0.5)
f32 = jnp.float32
bf16 = jnp.bfloat16


def attend(queries, latent_cache, lengths, latent_width):
    scores = (
        jnp.einsum("rhe,rje->rhj", queries, latent_cache, preferred_element_type=f32)
        * score_scale
    )
    alive_mask = lax.broadcasted_iota(jnp.int32, scores.shape, 2) < lengths[:, None, None]
    scores = jnp.where(alive_mask, scores, -1e30)
    row_max = jnp.max(scores, axis=2, keepdims=True)
    powers = jnp.exp(scores - row_max)
    weights = (powers / jnp.sum(powers, axis=2, keepdims=True)).astype(bf16)
    mixture = jnp.einsum("rhj,rje->rhe", weights, latent_cache, preferred_element_type=f32)
    return mixture[:, :, :latent_width].astype(bf16)


def local(queries, latent_cache, lengths, value_weight, output_weight):
    nx, nz, ny, nc = (lax.axis_size(a) for a in ("x", "z", "y", "c"))
    x, c = lax.axis_index("x"), lax.axis_index("c")
    requests = queries.shape[0]
    blocks = [output_weight] + [
        lax.ppermute(output_weight, "x", [(i, (i + k) % nx) for i in range(nx)])
        for k in range(1, nx)
    ]
    latent = attend(queries, latent_cache, lengths, value_weight.shape[1])
    swapped = lax.all_to_all(latent, ("y", "c"), split_axis=1, concat_axis=0, tiled=True)
    values = jnp.einsum("qhd,hde->qhe", swapped, value_weight, preferred_element_type=f32)
    values = values.astype(bf16).reshape(ny, nc, requests, -1)
    values = values.transpose(1, 0, 2, 3).reshape(nc, ny * requests, -1)
    everyone = lax.all_to_all(
        jnp.broadcast_to(values[None], (nz, *values.shape)), "z", split_axis=0, concat_axis=0, tiled=True
    )

    def product(core):
        rows = lax.dynamic_index_in_dim(everyone, core, 1, keepdims=False)
        rows = rows.reshape(nz * ny * requests, -1)
        return jnp.concatenate(
            [jnp.dot(rows, w, preferred_element_type=f32) for w in blocks], axis=1
        )

    theirs = product(1 - c)
    received = lax.ppermute(theirs, "c", [(i, (i + 1) % nc) for i in range(nc)])
    summed = (product(c) + received).astype(bf16).reshape(nz * ny, requests, -1)
    parts = lax.all_to_all(summed, ("z", "y"), split_axis=0, concat_axis=0, tiled=True)
    parts = parts.reshape(nz, ny, requests, nx, -1).astype(f32)
    total = jnp.sum(parts, axis=1).astype(bf16)
    order = jnp.mod(x - jnp.arange(nx), nx)
    total = jnp.take(total, order, axis=2)
    return total.transpose(1, 2, 0, 3).reshape(requests, -1)


def solution(mesh):
    grid = Mesh(mesh.devices.reshape(4, 8, 8, 2), ("x", "z", "y", "c"))
    everything = ("x", "z", "y", "c")
    return jax.shard_map(
        local,
        mesh=grid,
        in_specs=(
            P(everything, None, None),
            P(everything, None, None),
            P(everything),
            P(("y", "c"), None, None),
            P(("y", "c"), ("x", "z")),
        ),
        out_specs=P(everything, None),
        check_vma=False,
    )
```

```python
import jax
import jax.numpy as jnp
from jax import lax
from jax.sharding import Mesh
from jax.sharding import PartitionSpec as P

score_scale = 192.0 ** (-0.5)
f32 = jnp.float32
bf16 = jnp.bfloat16


def attend(queries, latent_cache, lengths, latent_width):
    scores = (
        jnp.einsum("rhe,rje->rhj", queries, latent_cache, preferred_element_type=f32)
        * score_scale
    )
    alive_mask = lax.broadcasted_iota(jnp.int32, scores.shape, 2) < lengths[:, None, None]
    scores = jnp.where(alive_mask, scores, -1e30)
    row_max = jnp.max(scores, axis=2, keepdims=True)
    powers = jnp.exp(scores - row_max)
    weights = (powers / jnp.sum(powers, axis=2, keepdims=True)).astype(bf16)
    mixture = jnp.einsum("rhj,rje->rhe", weights, latent_cache, preferred_element_type=f32)
    return mixture[:, :, :latent_width].astype(bf16)


def local(queries, latent_cache, lengths, value_weight, output_weight):
    nx, nz, ny, nc = (lax.axis_size(a) for a in ("x", "z", "y", "c"))
    x, c = lax.axis_index("x"), lax.axis_index("c")
    requests = queries.shape[0]
    ahead = [(i, (i + 1) % nx) for i in range(nx)]
    back = [(i, (i - 1) % nx) for i in range(nx)]
    half = output_weight.shape[1] // 2
    previous = lax.ppermute(output_weight, "x", ahead)
    following = lax.ppermute(output_weight, "x", back)
    latent = attend(queries, latent_cache, lengths, value_weight.shape[1])
    swapped = lax.all_to_all(latent, ("y", "c"), split_axis=1, concat_axis=0, tiled=True)
    values = jnp.einsum("qhd,hde->qhe", swapped, value_weight, preferred_element_type=f32)
    values = values.astype(bf16).reshape(ny, nc, requests, -1)
    values = values.transpose(1, 0, 2, 3).reshape(nc, ny * requests, -1)
    values, previous, following = lax.optimization_barrier((values, previous, following))
    low = lax.ppermute(previous[:, :half], "x", ahead)
    high = lax.ppermute(following[:, half:], "x", back)
    blocks = [output_weight, previous, low, high, following]
    everyone = lax.all_to_all(
        jnp.broadcast_to(values[None], (nz, *values.shape)), "z", split_axis=0, concat_axis=0, tiled=True
    )

    def product(core):
        rows = lax.dynamic_index_in_dim(everyone, core, 1, keepdims=False)
        rows = rows.reshape(nz * ny * requests, -1)
        return jnp.concatenate(
            [jnp.dot(rows, w, preferred_element_type=f32) for w in blocks], axis=1
        )

    theirs = product(1 - c)
    received = lax.ppermute(theirs, "c", [(i, (i + 1) % nc) for i in range(nc)])
    summed = (product(c) + received).astype(bf16).reshape(nz * ny, requests, -1)
    parts = lax.all_to_all(summed, ("z", "y"), split_axis=0, concat_axis=0, tiled=True)
    parts = parts.reshape(nz, ny, requests, nx, -1).astype(f32)
    total = jnp.sum(parts, axis=1).astype(bf16)
    order = jnp.mod(x - jnp.arange(nx), nx)
    total = jnp.take(total, order, axis=2)
    return total.transpose(1, 2, 0, 3).reshape(requests, -1)


def solution(mesh):
    grid = Mesh(mesh.devices.reshape(4, 8, 8, 2), ("x", "z", "y", "c"))
    everything = ("x", "z", "y", "c")
    return jax.shard_map(
        local,
        mesh=grid,
        in_specs=(
            P(everything, None, None),
            P(everything, None, None),
            P(everything),
            P(("y", "c"), None, None),
            P(("y", "c"), ("x", "z")),
        ),
        out_specs=P(everything, None),
        check_vma=False,
    )
```

```python
import jax
import jax.numpy as jnp
from jax import lax
from jax.sharding import Mesh
from jax.sharding import PartitionSpec as P

score_scale = 192.0 ** (-0.5)
f32 = jnp.float32
bf16 = jnp.bfloat16


def attend(queries, latent_cache, lengths, latent_width):
    scores = (
        jnp.einsum("rhe,rje->rhj", queries, latent_cache, preferred_element_type=f32)
        * score_scale
    )
    alive_mask = lax.broadcasted_iota(jnp.int32, scores.shape, 2) < lengths[:, None, None]
    scores = jnp.where(alive_mask, scores, -1e30)
    row_max = jnp.max(scores, axis=2, keepdims=True)
    powers = jnp.exp(scores - row_max)
    weights = (powers / jnp.sum(powers, axis=2, keepdims=True)).astype(bf16)
    mixture = jnp.einsum("rhj,rje->rhe", weights, latent_cache, preferred_element_type=f32)
    return mixture[:, :, :latent_width].astype(bf16)


def local(queries, latent_cache, lengths, value_weight, output_weight):
    nx, nz, ny, nc = (lax.axis_size(a) for a in ("x", "z", "y", "c"))
    x, c = lax.axis_index("x"), lax.axis_index("c")
    requests = queries.shape[0]
    weight = output_weight.T
    ahead = [(i, (i + 1) % nx) for i in range(nx)]
    back = [(i, (i - 1) % nx) for i in range(nx)]
    n = weight.shape[0]
    half, rest = n // 2, 2 * n // 7
    first = n - rest
    previous = lax.ppermute(weight[:first], "x", ahead)
    following = lax.ppermute(weight[rest:], "x", back)
    latent = attend(queries, latent_cache, lengths, value_weight.shape[1])
    swapped = lax.all_to_all(latent, ("y", "c"), split_axis=1, concat_axis=0, tiled=True)
    values = jnp.einsum("qhd,hde->qhe", swapped, value_weight, preferred_element_type=f32)
    values = values.astype(bf16).reshape(ny, nc, requests, -1)
    values = values.transpose(1, 0, 2, 3).reshape(nc, ny * requests, -1)
    values, previous, following = lax.optimization_barrier((values, previous, following))
    low = lax.ppermute(jnp.concatenate([weight[first:], previous[:half]]), "x", ahead)
    high = lax.ppermute(jnp.concatenate([following[half - rest :], weight[:rest]]), "x", back)
    blocks = [weight, previous, low, high, following]
    everyone = lax.all_to_all(
        jnp.broadcast_to(values[None], (nz, *values.shape)), "z", split_axis=0, concat_axis=0, tiled=True
    )

    def product(core):
        rows = lax.dynamic_index_in_dim(everyone, core, 1, keepdims=False)
        rows = rows.reshape(nz * ny * requests, -1)
        return jnp.concatenate(
            [jnp.einsum("rk,nk->rn", rows, w, preferred_element_type=f32) for w in blocks], axis=1
        )

    theirs = product(1 - c)
    received = lax.ppermute(theirs, "c", [(i, (i + 1) % nc) for i in range(nc)])
    summed = (product(c) + received).astype(bf16).reshape(nz * ny, requests, -1)
    parts = lax.all_to_all(summed, ("z", "y"), split_axis=0, concat_axis=0, tiled=True)
    parts = parts.reshape(nz, ny, requests, nx, -1).astype(f32)
    total = parts[:, 0]
    for i in range(1, ny):
        total = total + parts[:, i]
    total = total.astype(bf16).transpose(2, 1, 0, 3)
    total = jnp.concatenate([total[:1], total[:0:-1]])
    total = jnp.concatenate([total, total])
    total = lax.dynamic_slice_in_dim(total, jnp.mod(-x, nx), nx, 0)
    return total.transpose(1, 0, 2, 3).reshape(requests, -1)


def solution(mesh):
    grid = Mesh(mesh.devices.reshape(4, 8, 8, 2), ("x", "z", "y", "c"))
    everything = ("x", "z", "y", "c")
    return jax.shard_map(
        local,
        mesh=grid,
        in_specs=(
            P(everything, None, None),
            P(everything, None, None),
            P(everything),
            P(("y", "c"), None, None),
            P(("y", "c"), ("x", "z")),
        ),
        out_specs=P(everything, None),
        check_vma=False,
    )
```

```python
import jax
import jax.numpy as jnp
from jax import lax
from jax.sharding import Mesh
from jax.sharding import PartitionSpec as P

score_scale = 192.0 ** (-0.5)
f32 = jnp.float32
bf16 = jnp.bfloat16


def attend(queries, latent_cache, lengths, latent_width):
    scores = (
        jnp.einsum("rhe,rje->rhj", queries, latent_cache, preferred_element_type=f32)
        * score_scale
    )
    alive_mask = lax.broadcasted_iota(jnp.int32, scores.shape, 2) < lengths[:, None, None]
    scores = jnp.where(alive_mask, scores, -1e30)
    row_max = jnp.max(scores, axis=2, keepdims=True)
    powers = jnp.exp(scores - row_max)
    weights = (powers / jnp.sum(powers, axis=2, keepdims=True)).astype(bf16)
    mixture = jnp.einsum("rhj,rje->rhe", weights, latent_cache, preferred_element_type=f32)
    return mixture[:, :, :latent_width].astype(bf16)


def local(queries, latent_cache, lengths, value_weight, output_weight):
    nx, nz, ny, nc = (lax.axis_size(a) for a in ("x", "z", "y", "c"))
    x, c = lax.axis_index("x"), lax.axis_index("c")
    requests = queries.shape[0]
    others = [
        lax.ppermute(output_weight, "x", [(i, (i + k) % nx) for i in range(nx)]) for k in range(1, nx)
    ]

    def make_values():
        latent = attend(queries, latent_cache, lengths, value_weight.shape[1])
        swapped = lax.all_to_all(latent, ("y", "c"), split_axis=1, concat_axis=0, tiled=True)
        values = jnp.einsum("qhd,hde->qhe", swapped, value_weight, preferred_element_type=f32)
        values = values.astype(bf16).reshape(ny, nc, requests, -1)
        return values.transpose(1, 0, 2, 3).reshape(nc, ny * requests, -1)

    values = lax.cond(
        lengths[0] >= 1, make_values, lambda: jnp.zeros((nc, ny * requests, value_weight.shape[0] * value_weight.shape[2]), bf16)
    )
    values, others = lax.optimization_barrier((values, others))
    blocks = [output_weight, *others]
    everyone = lax.all_to_all(
        jnp.broadcast_to(values[None], (nz, *values.shape)), "z", split_axis=0, concat_axis=0, tiled=True
    )

    def product(core):
        rows = lax.dynamic_index_in_dim(everyone, core, 1, keepdims=False)
        rows = rows.reshape(nz * ny * requests, -1)
        return jnp.concatenate(
            [jnp.dot(rows, w, preferred_element_type=f32) for w in blocks], axis=1
        )

    theirs = product(1 - c)
    received = lax.ppermute(theirs, "c", [(i, (i + 1) % nc) for i in range(nc)])
    summed = (product(c) + received).astype(bf16).reshape(nz * ny, requests, -1)
    parts = lax.all_to_all(summed, ("z", "y"), split_axis=0, concat_axis=0, tiled=True)
    parts = parts.reshape(nz, ny, requests, nx, -1).astype(f32)
    total = parts[:, 0]
    for i in range(1, ny):
        total = total + parts[:, i]
    total = total.astype(bf16).transpose(2, 1, 0, 3)
    total = jnp.concatenate([total[:1], total[:0:-1]])
    total = jnp.concatenate([total, total])
    total = lax.dynamic_slice_in_dim(total, jnp.mod(-x, nx), nx, 0)
    return total.transpose(1, 0, 2, 3).reshape(requests, -1)


def solution(mesh):
    grid = Mesh(mesh.devices.reshape(4, 8, 8, 2), ("x", "z", "y", "c"))
    everything = ("x", "z", "y", "c")
    return jax.shard_map(
        local,
        mesh=grid,
        in_specs=(
            P(everything, None, None),
            P(everything, None, None),
            P(everything),
            P(("y", "c"), None, None),
            P(("y", "c"), ("x", "z")),
        ),
        out_specs=P(everything, None),
        check_vma=False,
    )
```

```python
import jax
import jax.numpy as jnp
from jax import lax
from jax.sharding import Mesh
from jax.sharding import PartitionSpec as P

score_scale = 192.0 ** (-0.5)
f32 = jnp.float32
bf16 = jnp.bfloat16


def attend(queries, latent_cache, lengths, latent_width):
    scores = (
        jnp.einsum("rhe,rje->rhj", queries, latent_cache, preferred_element_type=f32)
        * score_scale
    )
    alive_mask = lax.broadcasted_iota(jnp.int32, scores.shape, 2) < lengths[:, None, None]
    scores = jnp.where(alive_mask, scores, -1e30)
    row_max = jnp.max(scores, axis=2, keepdims=True)
    powers = jnp.exp(scores - row_max)
    weights = (powers / jnp.sum(powers, axis=2, keepdims=True)).astype(bf16)
    mixture = jnp.einsum("rhj,rje->rhe", weights, latent_cache, preferred_element_type=f32)
    return mixture[:, :, :latent_width].astype(bf16)


def local(queries, latent_cache, lengths, value_weight, output_weight):
    nx, nz, ny, nc = (lax.axis_size(a) for a in ("x", "z", "y", "c"))
    x, c = lax.axis_index("x"), lax.axis_index("c")
    requests = queries.shape[0]
    others = [
        lax.ppermute(output_weight, "x", [(i, (i + k) % nx) for i in range(nx)]) for k in range(1, nx)
    ]
    latent = attend(queries, latent_cache, lengths, value_weight.shape[1])
    swapped = lax.all_to_all(latent, ("y", "c"), split_axis=1, concat_axis=0, tiled=True)

    def gather_values():
        values = jnp.einsum("qhd,hde->qhe", swapped, value_weight, preferred_element_type=f32)
        values = values.astype(bf16).reshape(ny, nc, requests, -1)
        values = values.transpose(1, 0, 2, 3).reshape(nc, ny * requests, -1)
        values = jnp.broadcast_to(values[None], (nz, *values.shape))
        return lax.all_to_all(values, "z", split_axis=0, concat_axis=0, tiled=True)

    width = value_weight.shape[0] * value_weight.shape[2]
    everyone = lax.cond(
        lengths[0] >= 1, gather_values, lambda: jnp.zeros((nz, nc, ny * requests, width), bf16)
    )
    everyone, others = lax.optimization_barrier((everyone, others))
    blocks = [output_weight, *others]

    def product(core):
        rows = lax.dynamic_index_in_dim(everyone, core, 1, keepdims=False)
        rows = rows.reshape(nz * ny * requests, -1)
        return jnp.concatenate(
            [jnp.dot(rows, w, preferred_element_type=f32) for w in blocks], axis=1
        )

    theirs = product(1 - c)
    received = lax.ppermute(theirs, "c", [(i, (i + 1) % nc) for i in range(nc)])
    summed = (product(c) + received).astype(bf16).reshape(nz * ny, requests, -1)
    parts = lax.all_to_all(summed, ("z", "y"), split_axis=0, concat_axis=0, tiled=True)
    parts = parts.reshape(nz, ny, requests, nx, -1).astype(f32)
    total = parts[:, 0]
    for i in range(1, ny):
        total = total + parts[:, i]
    total = total.astype(bf16).transpose(2, 1, 0, 3)
    total = jnp.concatenate([total[:1], total[:0:-1]])
    total = jnp.concatenate([total, total])
    total = lax.dynamic_slice_in_dim(total, jnp.mod(-x, nx), nx, 0)
    return total.transpose(1, 0, 2, 3).reshape(requests, -1)


def solution(mesh):
    grid = Mesh(mesh.devices.reshape(4, 8, 8, 2), ("x", "z", "y", "c"))
    everything = ("x", "z", "y", "c")
    return jax.shard_map(
        local,
        mesh=grid,
        in_specs=(
            P(everything, None, None),
            P(everything, None, None),
            P(everything),
            P(("y", "c"), None, None),
            P(("y", "c"), ("x", "z")),
        ),
        out_specs=P(everything, None),
        check_vma=False,
    )
```

```python
import jax
import jax.numpy as jnp
from jax import lax
from jax.experimental import pallas as pl
from jax.experimental.pallas import tpu as pltpu
from jax.sharding import Mesh
from jax.sharding import PartitionSpec as P

score_scale = 192.0 ** (-0.5)
f32 = jnp.float32
bf16 = jnp.bfloat16


def attend_kernel(lengths, queries, cache, latent):
    live = lengths[pl.program_id(0)]
    keys = cache[0]
    scores = (
        lax.dot_general(queries[0], keys, (((0,), (0,)), ((), ())), preferred_element_type=f32)
        * score_scale
    )
    alive = lax.broadcasted_iota(jnp.int32, scores.shape, 1) < live
    scores = jnp.where(alive, scores, -1e30)
    powers = jnp.exp(scores - jnp.max(scores, axis=1, keepdims=True))
    weights = (powers / jnp.sum(powers, axis=1, keepdims=True)).astype(bf16)
    groups, _, heads, width = latent.shape
    mixture = lax.dot_general(
        weights, keys[:width], (((1,), (1,)), ((), ())), preferred_element_type=f32
    )
    latent[...] = mixture.reshape(groups, 1, heads, width).astype(bf16)


def attend(queries, cache, lengths, groups, width):
    requests, entries, heads = queries.shape
    slots = cache.shape[2]
    return pl.pallas_call(
        attend_kernel,
        grid_spec=pltpu.PrefetchScalarGridSpec(
            num_scalar_prefetch=1,
            grid=(requests,),
            in_specs=[
                pl.BlockSpec((1, entries, heads), lambda r, _: (r, 0, 0)),
                pl.BlockSpec((1, entries, slots), lambda r, _: (r, 0, 0)),
            ],
            out_specs=pl.BlockSpec((groups, 1, heads // groups, width), lambda r, _: (0, r, 0, 0)),
        ),
        out_shape=jax.ShapeDtypeStruct((groups, requests, heads // groups, width), bf16),
        cost_estimate=pl.CostEstimate(
            flops=2 * requests * heads * slots * (entries + width),
            transcendentals=requests * heads * slots,
            bytes_accessed=2 * requests * (entries * (heads + slots) + heads * width),
        ),
        name="attend",
    )(lengths, queries, cache)


def finish_kernel(place, parts, out):
    nz, nx = parts.shape[0], 4
    n = parts.shape[-1] // nx
    total = parts[:, 0].astype(f32)
    for i in range(1, parts.shape[1]):
        total = total + parts[:, i].astype(f32)
    columns = []
    for at in range(nx):
        k = lax.rem(place[0] + nx - at, nx)
        block = total[:, :, :n]
        for i in range(1, nx):
            block = jnp.where(k == i, total[:, :, i * n : (i + 1) * n], block)
        columns += [block[z] for z in range(nz)]
    out[...] = jnp.concatenate(columns, axis=1).astype(bf16)


def local(queries, latent_cache, lengths, value_weight, output_weight):
    nx, nz, ny, nc = (lax.axis_size(a) for a in ("x", "z", "y", "c"))
    x, c = lax.axis_index("x"), lax.axis_index("c")
    requests = queries.shape[0]
    others = [
        lax.ppermute(output_weight, "x", [(i, (i + k) % nx) for i in range(nx)]) for k in range(1, nx)
    ]
    latent = attend(
        queries.transpose(0, 2, 1), latent_cache.transpose(0, 2, 1), lengths, ny * nc, value_weight.shape[1]
    )
    swapped = lax.all_to_all(latent, ("y", "c"), split_axis=0, concat_axis=0, tiled=True)
    values = jnp.einsum("trhd,hde->trhe", swapped, value_weight, preferred_element_type=f32)
    values = values.astype(bf16).reshape(ny, nc, requests, -1)
    values = values.transpose(1, 0, 2, 3).reshape(nc, ny * requests, -1)

    def gather(values):
        values = jnp.broadcast_to(values[None], (nz, *values.shape))
        return lax.all_to_all(values, "z", split_axis=0, concat_axis=0, tiled=True)

    everyone = lax.cond(x < nx, gather, lambda v: jnp.zeros((nz, *v.shape), bf16), values)
    everyone, others = lax.optimization_barrier((everyone, others))
    blocks = [output_weight, *others]

    def product(core):
        rows = lax.dynamic_index_in_dim(everyone, core, 1, keepdims=False)
        rows = rows.reshape(nz * ny * requests, -1)
        return jnp.concatenate([jnp.dot(rows, w, preferred_element_type=f32) for w in blocks], axis=1)

    theirs = product(1 - c)
    received = lax.ppermute(theirs, "c", [(i, (i + 1) % nc) for i in range(nc)])
    summed = (product(c) + received).astype(bf16).reshape(nz * ny, requests, -1)
    summed, x = lax.optimization_barrier((summed, x))
    parts = lax.all_to_all(summed, ("z", "y"), split_axis=0, concat_axis=0, tiled=True)
    return pl.pallas_call(
        finish_kernel,
        grid_spec=pltpu.PrefetchScalarGridSpec(num_scalar_prefetch=1, grid=()),
        out_shape=jax.ShapeDtypeStruct((requests, nz * summed.shape[2]), bf16),
        name="finish",
    )(x.reshape(1), parts.reshape(nz, ny, requests, -1))


def solution(mesh):
    grid = Mesh(mesh.devices.reshape(4, 8, 8, 2), ("x", "z", "y", "c"))
    everything = ("x", "z", "y", "c")
    return jax.shard_map(
        local,
        mesh=grid,
        in_specs=(
            P(everything, None, None),
            P(everything, None, None),
            P(everything),
            P(("y", "c"), None, None),
            P(("y", "c"), ("x", "z")),
        ),
        out_specs=P(everything, None),
        check_vma=False,
    )
```

```python
import jax
import jax.numpy as jnp
from jax import lax
from jax.experimental import pallas as pl
from jax.experimental.pallas import tpu as pltpu
from jax.sharding import Mesh
from jax.sharding import PartitionSpec as P

score_scale = 192.0 ** (-0.5)
f32 = jnp.float32
bf16 = jnp.bfloat16


def attend_kernel(lengths, queries, cache, latent, near_queries, near_cache, near_latent, arrived, left):
    requests = near_queries.shape[0]
    groups, _, heads, width = near_latent.shape
    pairs = ((queries, near_queries), (cache, near_cache))
    loads = [
        [pltpu.make_async_copy(far.at[r], near.at[r], arrived.at[i, r]) for i, (far, near) in enumerate(pairs)]
        for r in range(requests)
    ]
    for load in loads:
        for copy in load:
            copy.start()
    scores = []
    for r in range(requests):
        for copy in loads[r]:
            copy.wait()
        raw = lax.dot_general(
            near_queries[r], near_cache[r], (((0,), (0,)), ((), ())), preferred_element_type=f32
        )
        scores.append(raw * score_scale)
    stores = []
    for r in range(requests):
        alive = lax.broadcasted_iota(jnp.int32, scores[r].shape, 1) < lengths[r]
        masked = jnp.where(alive, scores[r], -1e30)
        powers = jnp.exp(masked - jnp.max(masked, axis=1, keepdims=True))
        weights = (powers / jnp.sum(powers, axis=1, keepdims=True)).astype(bf16)
        mixture = lax.dot_general(
            weights, near_cache[r, :width], (((1,), (1,)), ((), ())), preferred_element_type=f32
        )
        near_latent[:, r] = mixture.reshape(groups, heads, width).astype(bf16)
        stores.append(pltpu.make_async_copy(near_latent.at[:, r], latent.at[:, r], left.at[r]))
        stores[r].start()
    for store in stores:
        store.wait()


def attend(queries, cache, lengths, groups, width):
    requests, entries, heads = queries.shape
    slots = cache.shape[2]
    shape = (groups, requests, heads // groups, width)
    anywhere = pl.BlockSpec(memory_space=pl.ANY)
    return pl.pallas_call(
        attend_kernel,
        in_specs=[pl.BlockSpec(memory_space=pltpu.SMEM), anywhere, anywhere],
        out_specs=anywhere,
        out_shape=jax.ShapeDtypeStruct(shape, bf16),
        scratch_shapes=[
            pltpu.VMEM(queries.shape, bf16),
            pltpu.VMEM(cache.shape, bf16),
            pltpu.VMEM(shape, bf16),
            pltpu.SemaphoreType.DMA((2, requests)),
            pltpu.SemaphoreType.DMA((requests,)),
        ],
        cost_estimate=pl.CostEstimate(
            flops=2 * requests * heads * slots * (entries + width),
            transcendentals=requests * heads * slots,
            bytes_accessed=2 * requests * (entries * (heads + slots) + heads * width),
        ),
        name="attend",
    )(lengths, queries, cache)


def finish_kernel(place, total, out):
    nz, nx = total.shape[0], 4
    n = total.shape[-1] // nx
    blocks = [total[:, :, i * n : (i + 1) * n] for i in range(nx)]
    columns = []
    for at in range(nx):
        k = lax.rem(place[0] + nx - at, nx)
        block = blocks[0]
        for i in range(1, nx):
            block = jnp.where(k == i, blocks[i], block)
        columns += [block[z] for z in range(nz)]
    out[...] = jnp.concatenate(columns, axis=1).astype(bf16)


def local(queries, latent_cache, lengths, value_weight, output_weight):
    nx, nz, ny, nc = (lax.axis_size(a) for a in ("x", "z", "y", "c"))
    x, c = lax.axis_index("x"), lax.axis_index("c")
    requests = queries.shape[0]
    others = [
        lax.ppermute(output_weight, "x", [(i, (i + k) % nx) for i in range(nx)]) for k in range(1, nx)
    ]
    latent = attend(
        queries.transpose(0, 2, 1), latent_cache.transpose(0, 2, 1), lengths, ny * nc, value_weight.shape[1]
    )
    swapped = lax.all_to_all(latent, ("y", "c"), split_axis=0, concat_axis=0, tiled=True)
    values = jnp.einsum("trhd,hde->trhe", swapped, value_weight, preferred_element_type=f32)
    values = values.astype(bf16).reshape(ny, nc, requests, -1)
    values = values.transpose(1, 0, 2, 3).reshape(nc, ny * requests, -1)

    def gather(values):
        values = jnp.broadcast_to(values[None], (nz, *values.shape))
        return lax.all_to_all(values, "z", split_axis=0, concat_axis=0, tiled=True)

    everyone = lax.cond(x < nx, gather, lambda v: jnp.zeros((nz, *v.shape), bf16), values)
    everyone, others = lax.optimization_barrier((everyone, others))
    blocks = [output_weight, *others]

    def product(core):
        rows = lax.dynamic_index_in_dim(everyone, core, 1, keepdims=False)
        rows = rows.reshape(nz * ny * requests, -1)
        return jnp.concatenate([jnp.dot(rows, w, preferred_element_type=f32) for w in blocks], axis=1)

    received = lax.ppermute(product(1 - c), "c", [(i, (i + 1) % nc) for i in range(nc)])
    mine = product(c)
    summed = (mine + received).astype(bf16).reshape(nz * ny, requests, -1)
    summed, x = lax.optimization_barrier((summed, x))
    parts = lax.all_to_all(summed, ("z", "y"), split_axis=0, concat_axis=0, tiled=True)
    parts = lax.optimization_barrier(parts.astype(f32))
    total = jnp.sum(parts.reshape(nz, ny, requests, -1), axis=1)
    return pl.pallas_call(
        finish_kernel,
        in_specs=[pl.BlockSpec(memory_space=pltpu.SMEM), pl.BlockSpec(memory_space=pltpu.VMEM)],
        out_shape=jax.ShapeDtypeStruct((requests, nz * total.shape[2]), bf16),
        name="finish",
    )(x.reshape(1), total)


def solution(mesh):
    grid = Mesh(mesh.devices.reshape(4, 8, 8, 2), ("x", "z", "y", "c"))
    everything = ("x", "z", "y", "c")
    return jax.shard_map(
        local,
        mesh=grid,
        in_specs=(
            P(everything, None, None),
            P(everything, None, None),
            P(everything),
            P(("y", "c"), None, None),
            P(("y", "c"), ("x", "z")),
        ),
        out_specs=P(everything, None),
        check_vma=False,
    )
```

```python
import jax
import jax.numpy as jnp
from jax import lax
from jax.experimental import pallas as pl
from jax.experimental.pallas import tpu as pltpu
from jax.sharding import Mesh
from jax.sharding import PartitionSpec as P

score_scale = 192.0 ** (-0.5)
f32 = jnp.float32
bf16 = jnp.bfloat16


def attend_kernel(lengths, queries, cache, latent, near_queries, near_cache, near_latent, arrived, left):
    requests = near_queries.shape[0]
    groups, _, heads, width = near_latent.shape
    pairs = ((queries, near_queries), (cache, near_cache))
    loads = [
        [pltpu.make_async_copy(far.at[r], near.at[r], arrived.at[i, r]) for i, (far, near) in enumerate(pairs)]
        for r in range(requests)
    ]
    for load in loads:
        for copy in load:
            copy.start()
    scores = []
    for r in range(requests):
        for copy in loads[r]:
            copy.wait()
        raw = lax.dot_general(
            near_queries[r], near_cache[r], (((0,), (0,)), ((), ())), preferred_element_type=f32
        )
        scores.append(raw * score_scale)
    stores = []
    for r in range(requests):
        alive = lax.broadcasted_iota(jnp.int32, scores[r].shape, 1) < lengths[r]
        masked = jnp.where(alive, scores[r], -1e30)
        powers = jnp.exp(masked - jnp.max(masked, axis=1, keepdims=True))
        weights = (powers / jnp.sum(powers, axis=1, keepdims=True)).astype(bf16)
        mixture = lax.dot_general(
            weights, near_cache[r, :width], (((1,), (1,)), ((), ())), preferred_element_type=f32
        )
        near_latent[:, r] = mixture.reshape(groups, heads, width).astype(bf16)
        stores.append(pltpu.make_async_copy(near_latent.at[:, r], latent.at[:, r], left.at[r]))
        stores[r].start()
    for store in stores:
        store.wait()


def attend(queries, cache, lengths, groups, width):
    requests, entries, heads = queries.shape
    slots = cache.shape[2]
    shape = (groups, requests, heads // groups, width)
    anywhere = pl.BlockSpec(memory_space=pl.ANY)
    return pl.pallas_call(
        attend_kernel,
        in_specs=[pl.BlockSpec(memory_space=pltpu.SMEM), anywhere, anywhere],
        out_specs=anywhere,
        out_shape=jax.ShapeDtypeStruct(shape, bf16),
        scratch_shapes=[
            pltpu.VMEM(queries.shape, bf16),
            pltpu.VMEM(cache.shape, bf16),
            pltpu.VMEM(shape, bf16),
            pltpu.SemaphoreType.DMA((2, requests)),
            pltpu.SemaphoreType.DMA((requests,)),
        ],
        cost_estimate=pl.CostEstimate(
            flops=2 * requests * heads * slots * (entries + width),
            transcendentals=requests * heads * slots,
            bytes_accessed=2 * requests * (entries * (heads + slots) + heads * width),
        ),
        name="attend",
    )(lengths, queries, cache)


def local(queries, latent_cache, lengths, value_weight, output_weight):
    nx, nz, ny, nc = (lax.axis_size(a) for a in ("x", "z", "y", "c"))
    x, c = lax.axis_index("x"), lax.axis_index("c")
    requests = queries.shape[0]
    others = [
        lax.ppermute(output_weight, "x", [(i, (i + k) % nx) for i in range(nx)]) for k in range(1, nx)
    ]
    latent = attend(
        queries.transpose(0, 2, 1), latent_cache.transpose(0, 2, 1), lengths, ny * nc, value_weight.shape[1]
    )
    swapped = lax.all_to_all(latent, ("y", "c"), split_axis=0, concat_axis=0, tiled=True)
    values = jnp.einsum("trhd,hde->trhe", swapped, value_weight, preferred_element_type=f32)
    values = values.astype(bf16).reshape(ny, nc, requests, -1)
    values = values.transpose(1, 0, 2, 3).reshape(nc, ny * requests, -1)

    def gather(values):
        values = jnp.broadcast_to(values[None], (nz, *values.shape))
        return lax.all_to_all(values, "z", split_axis=0, concat_axis=0, tiled=True)

    everyone = lax.cond(x < nx, gather, lambda v: jnp.zeros((nz, *v.shape), bf16), values)
    everyone, others = lax.optimization_barrier((everyone, others))
    blocks = [output_weight, *others]


    def product(core):
        rows = lax.dynamic_index_in_dim(everyone, core, 1, keepdims=False)
        rows = rows.reshape(nz * ny * requests, -1)
        return jnp.concatenate([jnp.dot(rows, w, preferred_element_type=f32) for w in blocks], axis=1)

    received = lax.ppermute(product(1 - c), "c", [(i, (i + 1) % nc) for i in range(nc)])
    summed = (product(c) + received).astype(bf16).reshape(nz * ny, requests, -1)
    summed, turn = lax.optimization_barrier((summed, jnp.mod(nx - x, nx)))
    parts = lax.all_to_all(summed, ("z", "y"), split_axis=0, concat_axis=0, tiled=True)
    parts = parts.reshape(nz, ny, requests, nx, -1).astype(f32)
    total = parts[:, 0]
    for i in range(1, ny):
        total = total + parts[:, i]
    total = total.astype(bf16).transpose(1, 2, 0, 3)
    shifted = total[:, :1], total[:, :0:-1]
    total = jnp.concatenate([*shifted, *shifted], axis=1)
    total = lax.dynamic_slice_in_dim(total, turn, nx, 1, allow_negative_indices=False)
    return total.reshape(requests, -1)


def solution(mesh):
    grid = Mesh(mesh.devices.reshape(4, 8, 8, 2), ("x", "z", "y", "c"))
    everything = ("x", "z", "y", "c")
    return jax.shard_map(
        local,
        mesh=grid,
        in_specs=(
            P(everything, None, None),
            P(everything, None, None),
            P(everything),
            P(("y", "c"), None, None),
            P(("y", "c"), ("x", "z")),
        ),
        out_specs=P(everything, None),
        check_vma=False,
    )
```

```python
import jax
import jax.numpy as jnp
from jax import lax
from jax.experimental import pallas as pl
from jax.experimental.pallas import tpu as pltpu
from jax.sharding import Mesh
from jax.sharding import PartitionSpec as P

score_scale = 192.0 ** (-0.5)
f32 = jnp.float32
bf16 = jnp.bfloat16


def attend_kernel(lengths, queries, cache, latent, near_queries, near_cache, near_latent, arrived, left):
    requests = near_queries.shape[0]
    groups, _, heads, width = near_latent.shape
    pairs = ((queries, near_queries), (cache, near_cache))
    loads = [
        [pltpu.make_async_copy(far.at[r], near.at[r], arrived.at[i, r]) for i, (far, near) in enumerate(pairs)]
        for r in range(requests)
    ]
    for load in loads:
        for copy in load:
            copy.start()
    scores = []
    for r in range(requests):
        for copy in loads[r]:
            copy.wait()
        raw = lax.dot_general(
            near_queries[r], near_cache[r], (((0,), (0,)), ((), ())), preferred_element_type=f32
        )
        scores.append(raw * score_scale)
    stores = []
    for r in range(requests):
        alive = lax.broadcasted_iota(jnp.int32, scores[r].shape, 1) < lengths[r]
        masked = jnp.where(alive, scores[r], -1e30)
        powers = jnp.exp(masked - jnp.max(masked, axis=1, keepdims=True))
        weights = (powers / jnp.sum(powers, axis=1, keepdims=True)).astype(bf16)
        mixture = lax.dot_general(
            weights, near_cache[r, :width], (((1,), (1,)), ((), ())), preferred_element_type=f32
        )
        near_latent[:, r] = mixture.reshape(groups, heads, width).astype(bf16)
        stores.append(pltpu.make_async_copy(near_latent.at[:, r], latent.at[:, r], left.at[r]))
        stores[r].start()
    for store in stores:
        store.wait()


def attend(queries, cache, lengths, groups, width):
    requests, entries, heads = queries.shape
    slots = cache.shape[2]
    shape = (groups, requests, heads // groups, width)
    anywhere = pl.BlockSpec(memory_space=pl.ANY)
    return pl.pallas_call(
        attend_kernel,
        in_specs=[pl.BlockSpec(memory_space=pltpu.SMEM), anywhere, anywhere],
        out_specs=anywhere,
        out_shape=jax.ShapeDtypeStruct(shape, bf16),
        scratch_shapes=[
            pltpu.VMEM(queries.shape, bf16),
            pltpu.VMEM(cache.shape, bf16),
            pltpu.VMEM(shape, bf16),
            pltpu.SemaphoreType.DMA((2, requests)),
            pltpu.SemaphoreType.DMA((requests,)),
        ],
        cost_estimate=pl.CostEstimate(
            flops=2 * requests * heads * slots * (entries + width),
            transcendentals=requests * heads * slots,
            bytes_accessed=2 * requests * (entries * (heads + slots) + heads * width),
        ),
        name="attend",
    )(lengths, queries, cache)


def local(queries, latent_cache, lengths, value_weight, output_weight):
    nx, nz, ny, nc = (lax.axis_size(a) for a in ("x", "z", "y", "c"))
    x, c = lax.axis_index("x"), lax.axis_index("c")
    requests = queries.shape[0]
    sent = {k: lax.ppermute(output_weight, "x", [(i, (i + k) % nx) for i in range(nx)]) for k in (1, 2, 3)}
    latent = attend(
        queries.transpose(0, 2, 1), latent_cache.transpose(0, 2, 1), lengths, ny * nc, value_weight.shape[1]
    )
    swapped = lax.all_to_all(latent, ("y", "c"), split_axis=0, concat_axis=0, tiled=True)
    values = jnp.einsum("trhd,hde->trhe", swapped, value_weight, preferred_element_type=f32)
    values = values.astype(bf16).reshape(ny, nc, requests, -1)
    values = values.transpose(1, 0, 2, 3).reshape(nc, ny * requests, -1)

    def gather(values):
        values = jnp.broadcast_to(values[None], (nz, *values.shape))
        return lax.all_to_all(values, "z", split_axis=0, concat_axis=0, tiled=True)

    everyone = lax.cond(x < nx, gather, lambda v: jnp.zeros((nz, *v.shape), bf16), values)
    everyone, *others = lax.optimization_barrier((everyone, sent[3], sent[1], sent[2]))
    sent = dict(zip((3,1,2), others))
    blocks = [output_weight, *(sent[k] for k in range(1, nx))]

    def product(core):
        rows = lax.dynamic_index_in_dim(everyone, core, 1, keepdims=False)
        rows = rows.reshape(nz * ny * requests, -1)
        return jnp.concatenate([jnp.dot(rows, w, preferred_element_type=f32) for w in blocks], axis=1)

    received = lax.ppermute(product(1 - c).astype(bf16), "c", [(i, (i + 1) % nc) for i in range(nc)])
    summed = (product(c) + received).astype(bf16).reshape(nz * ny, requests, -1)
    summed, turn = lax.optimization_barrier((summed, jnp.mod(nx - x, nx)))
    parts = lax.all_to_all(summed, ("z", "y"), split_axis=0, concat_axis=0, tiled=True)
    parts = parts.reshape(nz, ny, requests, nx, -1).astype(f32)
    total = parts[:, 0]
    for i in range(1, ny):
        total = total + parts[:, i]
    total = total.astype(bf16).transpose(1, 2, 0, 3)
    shifted = total[:, :1], total[:, :0:-1]
    total = jnp.concatenate([*shifted, *shifted], axis=1)
    total = lax.dynamic_slice_in_dim(total, turn, nx, 1, allow_negative_indices=False)
    return total.reshape(requests, -1)


def solution(mesh):
    grid = Mesh(mesh.devices.reshape(4, 8, 8, 2), ("x", "z", "y", "c"))
    everything = ("x", "z", "y", "c")
    return jax.shard_map(
        local,
        mesh=grid,
        in_specs=(
            P(everything, None, None),
            P(everything, None, None),
            P(everything),
            P(("y", "c"), None, None),
            P(("y", "c"), ("x", "z")),
        ),
        out_specs=P(everything, None),
        check_vma=False,
    )
```

```python
import jax
import jax.numpy as jnp
from jax import lax
from jax.experimental import pallas as pl
from jax.experimental.layout import Layout, with_layout_constraint
from jax.experimental.pallas import tpu as pltpu
from jax.sharding import Mesh
from jax.sharding import PartitionSpec as P

score_scale = 192.0 ** (-0.5)
f32 = jnp.float32
bf16 = jnp.bfloat16


def attend_kernel(lengths, queries, cache, latent, near_queries, near_cache, near_latent, arrived, left):
    requests = near_queries.shape[0]
    cores, groups, _, heads, width = near_latent.shape
    pairs = ((queries, near_queries), (cache, near_cache))
    loads = [
        [pltpu.make_async_copy(far.at[r], near.at[r], arrived.at[i, r]) for i, (far, near) in enumerate(pairs)]
        for r in range(requests)
    ]
    for load in loads:
        for copy in load:
            copy.start()
    scores = []
    for r in range(requests):
        for copy in loads[r]:
            copy.wait()
        raw = lax.dot_general(
            near_queries[r], near_cache[r], (((0,), (0,)), ((), ())), preferred_element_type=f32
        )
        scores.append(raw * score_scale)
    stores = []
    for r in range(requests):
        alive = lax.broadcasted_iota(jnp.int32, scores[r].shape, 1) < lengths[r]
        masked = jnp.where(alive, scores[r], -1e30)
        powers = jnp.exp(masked - jnp.max(masked, axis=1, keepdims=True))
        weights = (powers / jnp.sum(powers, axis=1, keepdims=True)).astype(bf16)
        mixture = lax.dot_general(
            weights, near_cache[r, :width], (((1,), (1,)), ((), ())), preferred_element_type=f32
        )
        mixture = mixture.reshape(groups, cores, heads, width).astype(bf16)
        for core in range(cores):
            near_latent[core, :, r] = mixture[:, core]
        stores.append(pltpu.make_async_copy(near_latent.at[:, :, r], latent.at[:, :, r], left.at[r]))
        stores[r].start()
    for store in stores:
        store.wait()


def attend(queries, cache, lengths, groups, cores, width):
    requests, entries, heads = queries.shape
    slots = cache.shape[2]
    shape = (cores, groups, requests, heads // (groups * cores), width)
    anywhere = pl.BlockSpec(memory_space=pl.ANY)
    return pl.pallas_call(
        attend_kernel,
        in_specs=[pl.BlockSpec(memory_space=pltpu.SMEM), anywhere, anywhere],
        out_specs=anywhere,
        out_shape=jax.ShapeDtypeStruct(shape, bf16),
        scratch_shapes=[
            pltpu.VMEM(queries.shape, bf16),
            pltpu.VMEM(cache.shape, bf16),
            pltpu.VMEM(shape, bf16),
            pltpu.SemaphoreType.DMA((2, requests)),
            pltpu.SemaphoreType.DMA((requests,)),
        ],
        cost_estimate=pl.CostEstimate(
            flops=2 * requests * heads * slots * (entries + width),
            transcendentals=requests * heads * slots,
            bytes_accessed=2 * requests * (entries * (heads + slots) + heads * width),
        ),
        name="attend",
    )(lengths, queries, cache)


def local(queries, latent_cache, lengths, value_weight, output_weight):
    nx, nz, ny, nc = (lax.axis_size(a) for a in ("x", "z", "y", "c"))
    x, c = lax.axis_index("x"), lax.axis_index("c")
    requests = queries.shape[0]
    others = [
        lax.ppermute(output_weight, "x", [(i, (i + k) % nx) for i in range(nx)]) for k in range(1, nx)
    ]
    latent = attend(
        queries.transpose(0, 2, 1), latent_cache.transpose(0, 2, 1), lengths, ny, nc, value_weight.shape[1]
    )
    latent = latent.reshape(nc * ny, *latent.shape[2:])
    swapped = lax.all_to_all(latent, ("c", "y"), split_axis=0, concat_axis=0, tiled=True)
    swapped = with_layout_constraint(swapped, Layout(major_to_minor=(0, 1, 2, 3)))
    values = jnp.einsum("trhd,hde->trhe", swapped, value_weight, preferred_element_type=f32)
    values = values.astype(bf16).reshape(nc, ny * requests, -1)

    def gather(values):
        values = jnp.broadcast_to(values[None], (nz, *values.shape))
        return lax.all_to_all(values, "z", split_axis=0, concat_axis=0, tiled=True)

    everyone = lax.cond(x < nx, gather, lambda v: jnp.zeros((nz, *v.shape), bf16), values)
    everyone, others = lax.optimization_barrier((everyone, others))
    blocks = [output_weight, *others]


    def product(core):
        rows = lax.dynamic_index_in_dim(everyone, core, 1, keepdims=False)
        rows = rows.reshape(nz * ny * requests, -1)
        return jnp.concatenate([jnp.dot(rows, w, preferred_element_type=f32) for w in blocks], axis=1)

    received = lax.ppermute(product(1 - c), "c", [(i, (i + 1) % nc) for i in range(nc)])
    summed = (product(c) + received).astype(bf16).reshape(nz, ny, requests, -1)
    summed = summed.transpose(1, 0, 2, 3).reshape(ny * nz, requests, -1)
    summed, turn = lax.optimization_barrier((summed, jnp.mod(nx - x, nx)))
    parts = lax.all_to_all(summed, ("y", "z"), split_axis=0, concat_axis=0, tiled=True)
    parts = parts.reshape(ny, nz, requests, nx, -1).astype(f32)
    total = parts[0]
    for i in range(1, ny):
        total = total + parts[i]
    total = total.astype(bf16).transpose(1, 2, 0, 3)
    shifted = total[:, :1], total[:, :0:-1]
    total = jnp.concatenate([*shifted, *shifted], axis=1)
    total = lax.dynamic_slice_in_dim(total, turn, nx, 1, allow_negative_indices=False)
    return total.reshape(requests, -1)


def solution(mesh):
    grid = Mesh(mesh.devices.reshape(4, 8, 8, 2), ("x", "z", "y", "c"))
    everything = ("x", "z", "y", "c")
    return jax.shard_map(
        local,
        mesh=grid,
        in_specs=(
            P(everything, None, None),
            P(everything, None, None),
            P(everything),
            P(("y", "c"), None, None),
            P(("y", "c"), ("x", "z")),
        ),
        out_specs=P(everything, None),
        check_vma=False,
    )
```

```python
import jax
import jax.numpy as jnp
from jax import lax
from jax.experimental import pallas as pl
from jax.experimental.layout import Layout, with_layout_constraint
from jax.experimental.pallas import tpu as pltpu
from jax.sharding import Mesh
from jax.sharding import PartitionSpec as P

score_scale = 192.0 ** (-0.5)
f32 = jnp.float32
bf16 = jnp.bfloat16


def attend_kernel(lengths, queries, cache, latent, near_queries, near_cache, near_latent, arrived, left):
    requests = near_queries.shape[0]
    cores, groups, _, heads, width = near_latent.shape
    pairs = ((queries, near_queries), (cache, near_cache))
    loads = [
        [pltpu.make_async_copy(far.at[r], near.at[r], arrived.at[i, r]) for i, (far, near) in enumerate(pairs)]
        for r in range(requests)
    ]
    for load in loads:
        for copy in load:
            copy.start()
    scores = []
    for r in range(requests):
        for copy in loads[r]:
            copy.wait()
        raw = lax.dot_general(
            near_queries[r], near_cache[r], (((0,), (0,)), ((), ())), preferred_element_type=f32
        )
        scores.append(raw * score_scale)
    stores = []
    for r in range(requests):
        alive = lax.broadcasted_iota(jnp.int32, scores[r].shape, 1) < lengths[r]
        masked = jnp.where(alive, scores[r], -1e30)
        powers = jnp.exp(masked - jnp.max(masked, axis=1, keepdims=True))
        weights = (powers / jnp.sum(powers, axis=1, keepdims=True)).astype(bf16)
        mixture = lax.dot_general(
            weights, near_cache[r, :width], (((1,), (1,)), ((), ())), preferred_element_type=f32
        )
        mixture = mixture.reshape(groups, cores, heads, width).astype(bf16)
        for core in range(cores):
            near_latent[core, :, r] = mixture[:, core]
        stores.append(pltpu.make_async_copy(near_latent.at[:, :, r], latent.at[:, :, r], left.at[r]))
        stores[r].start()
    for store in stores:
        store.wait()


def attend(queries, cache, lengths, groups, cores, width):
    requests, entries, heads = queries.shape
    slots = cache.shape[2]
    shape = (cores, groups, requests, heads // (groups * cores), width)
    anywhere = pl.BlockSpec(memory_space=pl.ANY)
    return pl.pallas_call(
        attend_kernel,
        in_specs=[pl.BlockSpec(memory_space=pltpu.SMEM), anywhere, anywhere],
        out_specs=anywhere,
        out_shape=jax.ShapeDtypeStruct(shape, bf16),
        scratch_shapes=[
            pltpu.VMEM(queries.shape, bf16),
            pltpu.VMEM(cache.shape, bf16),
            pltpu.VMEM(shape, bf16),
            pltpu.SemaphoreType.DMA((2, requests)),
            pltpu.SemaphoreType.DMA((requests,)),
        ],
        cost_estimate=pl.CostEstimate(
            flops=2 * requests * heads * slots * (entries + width),
            transcendentals=requests * heads * slots,
            bytes_accessed=2 * requests * (entries * (heads + slots) + heads * width),
        ),
        name="attend",
    )(lengths, queries, cache)


def local(queries, latent_cache, lengths, value_weight, output_weight):
    nx, nz, ny, nc = (lax.axis_size(a) for a in ("x", "z", "y", "c"))
    x, c = lax.axis_index("x"), lax.axis_index("c")
    requests = queries.shape[0]
    sent = {k: lax.ppermute(output_weight, "x", [(i, (i + k) % nx) for i in range(nx)]) for k in (1, 2, 3)}
    latent = attend(
        queries.transpose(0, 2, 1), latent_cache.transpose(0, 2, 1), lengths, ny, nc, value_weight.shape[1]
    )
    latent = latent.reshape(nc * ny, *latent.shape[2:])
    swapped = lax.all_to_all(latent, ("c", "y"), split_axis=0, concat_axis=0, tiled=True)
    swapped = with_layout_constraint(swapped, Layout(major_to_minor=(0, 1, 2, 3)))
    values = jnp.einsum("trhd,hde->trhe", swapped, value_weight, preferred_element_type=f32)
    values = values.astype(bf16).reshape(nc, ny * requests, -1)

    def gather(values):
        values = jnp.broadcast_to(values[None], (nz, *values.shape))
        return lax.all_to_all(values, "z", split_axis=0, concat_axis=0, tiled=True)

    everyone = lax.cond(x < nx, gather, lambda v: jnp.zeros((nz, *v.shape), bf16), values)
    blocks = [output_weight, *(sent[k] for k in range(1, nx))]

    def product(core, order=()):
        rows = lax.dynamic_index_in_dim(everyone, core, 1, keepdims=False)
        rows = rows.reshape(nz * ny * requests, -1)
        weights, outs = dict(enumerate(blocks)), {}
        for at, k in enumerate(order or weights):
            if order and at > 0:
                weights[k], outs[order[at - 1]] = lax.optimization_barrier((weights[k], outs[order[at - 1]]))
            outs[k] = jnp.dot(rows, weights[k], preferred_element_type=f32)
        return jnp.concatenate([outs[k] for k in weights], axis=1)

    received = lax.ppermute(product(1 - c, (0, 2, 3, 1)), "c", [(i, (i + 1) % nc) for i in range(nc)])
    summed = (product(c) + received).astype(bf16).reshape(nz, ny, requests, -1)
    summed = summed.transpose(1, 0, 2, 3).reshape(ny * nz, requests, -1)
    summed, turn = lax.optimization_barrier((summed, jnp.mod(nx - x, nx)))
    parts = lax.all_to_all(summed, ("y", "z"), split_axis=0, concat_axis=0, tiled=True)
    parts = parts.reshape(ny, nz, requests, nx, -1).astype(f32)
    total = parts[0]
    for i in range(1, ny):
        total = total + parts[i]
    total = total.astype(bf16).transpose(1, 2, 0, 3)
    shifted = total[:, :1], total[:, :0:-1]
    total = jnp.concatenate([*shifted, *shifted], axis=1)
    total = lax.dynamic_slice_in_dim(total, turn, nx, 1, allow_negative_indices=False)
    return total.reshape(requests, -1)


def solution(mesh):
    grid = Mesh(mesh.devices.reshape(4, 8, 8, 2), ("x", "z", "y", "c"))
    everything = ("x", "z", "y", "c")
    return jax.shard_map(
        local,
        mesh=grid,
        in_specs=(
            P(everything, None, None),
            P(everything, None, None),
            P(everything),
            P(("y", "c"), None, None),
            P(("y", "c"), ("x", "z")),
        ),
        out_specs=P(everything, None),
        check_vma=False,
    )
```

```python
import jax
import jax.numpy as jnp
from jax import lax
from jax.experimental import pallas as pl
from jax.experimental.layout import Layout, with_layout_constraint
from jax.experimental.pallas import tpu as pltpu
from jax.sharding import Mesh
from jax.sharding import PartitionSpec as P

score_scale = 192.0 ** (-0.5)
f32 = jnp.float32
bf16 = jnp.bfloat16


def attend_kernel(lengths, queries, cache, latent, near_queries, near_cache, near_latent, arrived, left):
    requests = near_queries.shape[0]
    cores, groups, _, heads, width = near_latent.shape
    pairs = ((queries, near_queries), (cache, near_cache))
    loads = [
        [pltpu.make_async_copy(far.at[r], near.at[r], arrived.at[i, r]) for i, (far, near) in enumerate(pairs)]
        for r in range(requests)
    ]
    for load in loads:
        for copy in load:
            copy.start()
    scores = []
    for r in range(requests):
        for copy in loads[r]:
            copy.wait()
        raw = lax.dot_general(
            near_queries[r], near_cache[r], (((0,), (0,)), ((), ())), preferred_element_type=f32
        )
        scores.append(raw * score_scale)
    stores = []
    for r in range(requests):
        alive = lax.broadcasted_iota(jnp.int32, scores[r].shape, 1) < lengths[r]
        masked = jnp.where(alive, scores[r], -1e30)
        powers = jnp.exp(masked - jnp.max(masked, axis=1, keepdims=True))
        weights = (powers / jnp.sum(powers, axis=1, keepdims=True)).astype(bf16)
        mixture = lax.dot_general(
            weights, near_cache[r, :width], (((1,), (1,)), ((), ())), preferred_element_type=f32
        )
        mixture = mixture.reshape(groups, cores, heads, width).astype(bf16)
        for core in range(cores):
            near_latent[core, :, r] = mixture[:, core]
        stores.append(pltpu.make_async_copy(near_latent.at[:, :, r], latent.at[:, :, r], left.at[r]))
        stores[r].start()
    for store in stores:
        store.wait()


def attend(queries, cache, lengths, groups, cores, width):
    requests, entries, heads = queries.shape
    slots = cache.shape[2]
    shape = (cores, groups, requests, heads // (groups * cores), width)
    anywhere = pl.BlockSpec(memory_space=pl.ANY)
    return pl.pallas_call(
        attend_kernel,
        in_specs=[pl.BlockSpec(memory_space=pltpu.SMEM), anywhere, anywhere],
        out_specs=anywhere,
        out_shape=jax.ShapeDtypeStruct(shape, bf16),
        scratch_shapes=[
            pltpu.VMEM(queries.shape, bf16),
            pltpu.VMEM(cache.shape, bf16),
            pltpu.VMEM(shape, bf16),
            pltpu.SemaphoreType.DMA((2, requests)),
            pltpu.SemaphoreType.DMA((requests,)),
        ],
        cost_estimate=pl.CostEstimate(
            flops=2 * requests * heads * slots * (entries + width),
            transcendentals=requests * heads * slots,
            bytes_accessed=2 * requests * (entries * (heads + slots) + heads * width),
        ),
        name="attend",
    )(lengths, queries, cache)


def local(queries, latent_cache, lengths, value_weight, output_weight):
    nx, nz, ny, nc = (lax.axis_size(a) for a in ("x", "z", "y", "c"))
    x, c = lax.axis_index("x"), lax.axis_index("c")
    requests = queries.shape[0]
    sent = {k: lax.ppermute(output_weight, "x", [(i, (i + k) % nx) for i in range(nx)]) for k in (1, 3, 2)}
    latent = attend(
        queries.transpose(0, 2, 1), latent_cache.transpose(0, 2, 1), lengths, ny, nc, value_weight.shape[1]
    )
    latent = latent.reshape(nc * ny, *latent.shape[2:])
    swapped = lax.all_to_all(latent, ("c", "y"), split_axis=0, concat_axis=0, tiled=True)
    swapped = with_layout_constraint(swapped, Layout(major_to_minor=(0, 1, 2, 3)))
    values = jnp.einsum("trhd,hde->trhe", swapped, value_weight, preferred_element_type=f32)
    values = values.astype(bf16).reshape(nc, ny * requests, -1)

    def gather(values):
        values = jnp.broadcast_to(values[None], (nz, *values.shape))
        return lax.all_to_all(values, "z", split_axis=0, concat_axis=0, tiled=True)

    everyone = lax.cond(x < nx, gather, lambda v: jnp.zeros((nz, *v.shape), bf16), values)
    everyone, *others = lax.optimization_barrier((everyone, *sent.values()))
    sent = dict(zip(sent, others))
    blocks = [output_weight, *(sent[k] for k in range(1, nx))]

    def product(core):
        rows = lax.dynamic_index_in_dim(everyone, core, 1, keepdims=False)
        rows = rows.reshape(nz * ny * requests, -1)
        return jnp.concatenate([jnp.dot(rows, w, preferred_element_type=f32) for w in blocks], axis=1)

    received = lax.ppermute(product(1 - c), "c", [(i, (i + 1) % nc) for i in range(nc)])
    summed = (product(c) + received).astype(bf16).reshape(nz * ny, requests, -1)
    summed, turn = lax.optimization_barrier((summed, jnp.mod(nx - x, nx)))
    parts = lax.all_to_all(summed, ("z", "y"), split_axis=0, concat_axis=0, tiled=True)
    parts = parts.reshape(nz, ny, requests, nx, -1).astype(f32)
    total = parts[:, 0]
    for i in range(1, ny):
        total = total + parts[:, i]
    total = total.astype(bf16).transpose(1, 2, 0, 3)
    shifted = total[:, :1], total[:, :0:-1]
    total = jnp.concatenate([*shifted, *shifted], axis=1)
    total = lax.dynamic_slice_in_dim(total, turn, nx, 1, allow_negative_indices=False)
    return total.reshape(requests, -1)


def solution(mesh):
    grid = Mesh(mesh.devices.reshape(4, 8, 8, 2), ("x", "z", "y", "c"))
    everything = ("x", "z", "y", "c")
    return jax.shard_map(
        local,
        mesh=grid,
        in_specs=(
            P(everything, None, None),
            P(everything, None, None),
            P(everything),
            P(("y", "c"), None, None),
            P(("y", "c"), ("x", "z")),
        ),
        out_specs=P(everything, None),
        check_vma=False,
    )
```

```python
import jax
import jax.numpy as jnp
from jax import lax
from jax.experimental import pallas as pl
from jax.experimental.layout import Layout, with_layout_constraint
from jax.experimental.pallas import tpu as pltpu
from jax.sharding import Mesh
from jax.sharding import PartitionSpec as P

score_scale = 192.0 ** (-0.5)
f32 = jnp.float32
bf16 = jnp.bfloat16


def attend_kernel(lengths, queries, cache, latent, near_queries, near_cache, near_latent, arrived, left):
    requests = near_queries.shape[0]
    cores, groups, _, heads, width = near_latent.shape
    pairs = ((queries, near_queries), (cache, near_cache))
    loads = [
        [pltpu.make_async_copy(far.at[r], near.at[r], arrived.at[i, r]) for i, (far, near) in enumerate(pairs)]
        for r in range(requests)
    ]
    for load in loads:
        for copy in load:
            copy.start()
    scores = []
    for r in range(requests):
        for copy in loads[r]:
            copy.wait()
        raw = lax.dot_general(
            near_queries[r], near_cache[r], (((0,), (0,)), ((), ())), preferred_element_type=f32
        )
        scores.append(raw * score_scale)
    stores = []
    for r in range(requests):
        alive = lax.broadcasted_iota(jnp.int32, scores[r].shape, 1) < lengths[r]
        masked = jnp.where(alive, scores[r], -1e30)
        powers = jnp.exp(masked - jnp.max(masked, axis=1, keepdims=True))
        weights = (powers / jnp.sum(powers, axis=1, keepdims=True)).astype(bf16)
        mixture = lax.dot_general(
            weights, near_cache[r, :width], (((1,), (1,)), ((), ())), preferred_element_type=f32
        )
        mixture = mixture.reshape(groups, cores, heads, width).astype(bf16)
        for core in range(cores):
            near_latent[core, :, r] = mixture[:, core]
        stores.append(pltpu.make_async_copy(near_latent.at[:, :, r], latent.at[:, :, r], left.at[r]))
        stores[r].start()
    for store in stores:
        store.wait()


def attend(queries, cache, lengths, groups, cores, width):
    requests, entries, heads = queries.shape
    slots = cache.shape[2]
    shape = (cores, groups, requests, heads // (groups * cores), width)
    anywhere = pl.BlockSpec(memory_space=pl.ANY)
    return pl.pallas_call(
        attend_kernel,
        in_specs=[pl.BlockSpec(memory_space=pltpu.SMEM), anywhere, anywhere],
        out_specs=anywhere,
        out_shape=jax.ShapeDtypeStruct(shape, bf16),
        scratch_shapes=[
            pltpu.VMEM(queries.shape, bf16),
            pltpu.VMEM(cache.shape, bf16),
            pltpu.VMEM(shape, bf16),
            pltpu.SemaphoreType.DMA((2, requests)),
            pltpu.SemaphoreType.DMA((requests,)),
        ],
        cost_estimate=pl.CostEstimate(
            flops=2 * requests * heads * slots * (entries + width),
            transcendentals=requests * heads * slots,
            bytes_accessed=2 * requests * (entries * (heads + slots) + heads * width),
        ),
        name="attend",
    )(lengths, queries, cache)


def local(queries, latent_cache, lengths, value_weight, output_weight):
    nx, nz, ny, nc = (lax.axis_size(a) for a in ("x", "z", "y", "c"))
    x, c = lax.axis_index("x"), lax.axis_index("c")
    requests = queries.shape[0]
    sent = {k: lax.ppermute(output_weight, "x", [(i, (i + k) % nx) for i in range(nx)]) for k in (1, 3, 2)}
    latent = attend(
        queries.transpose(0, 2, 1), latent_cache.transpose(0, 2, 1), lengths, ny, nc, value_weight.shape[1]
    )
    latent = latent.reshape(nc * ny, *latent.shape[2:])
    swapped = lax.all_to_all(latent, ("c", "y"), split_axis=0, concat_axis=0, tiled=True)
    swapped = with_layout_constraint(swapped, Layout(major_to_minor=(0, 1, 2, 3)))
    values = jnp.einsum("trhd,hde->trhe", swapped, value_weight, preferred_element_type=f32)
    values = values.astype(bf16).reshape(nc, ny * requests, -1)

    def gather(values):
        values = jnp.broadcast_to(values[None], (nz, *values.shape))
        return lax.all_to_all(
            values, "z", split_axis=0, concat_axis=0, tiled=True, axis_index_groups=[list(range(nz - 1, -1, -1))]
        )

    everyone = lax.cond(x < nx, gather, lambda v: jnp.zeros((nz, *v.shape), bf16), values)
    everyone, *others = lax.optimization_barrier((everyone, *sent.values()))
    sent = dict(zip(sent, others))
    blocks = [output_weight, *(sent[k] for k in range(1, nx))]

    def product(core):
        rows = lax.dynamic_index_in_dim(everyone, core, 1, keepdims=False)
        rows = rows.reshape(nz * ny * requests, -1)
        return jnp.concatenate([jnp.dot(rows, w, preferred_element_type=f32) for w in blocks], axis=1)

    received = lax.ppermute(product(1 - c), "c", [(i, (i + 1) % nc) for i in range(nc)])
    summed = (product(c) + received).astype(bf16).reshape(nz * ny, requests, -1)
    summed, turn = lax.optimization_barrier((summed, jnp.mod(nx - x, nx)))
    downward = [[z * ny + y for z in range(nz - 1, -1, -1) for y in range(ny)]]
    parts = lax.all_to_all(
        summed, ("z", "y"), split_axis=0, concat_axis=0, tiled=True, axis_index_groups=downward
    )
    parts = parts.reshape(nz, ny, requests, nx, -1).astype(f32)
    total = parts[:, 0]
    for i in range(1, ny):
        total = total + parts[:, i]
    total = total[::-1].astype(bf16).transpose(1, 2, 0, 3)
    shifted = total[:, :1], total[:, :0:-1]
    total = jnp.concatenate([*shifted, *shifted], axis=1)
    total = lax.dynamic_slice_in_dim(total, turn, nx, 1, allow_negative_indices=False)
    return total.reshape(requests, -1)


def solution(mesh):
    grid = Mesh(mesh.devices.reshape(4, 8, 8, 2), ("x", "z", "y", "c"))
    everything = ("x", "z", "y", "c")
    return jax.shard_map(
        local,
        mesh=grid,
        in_specs=(
            P(everything, None, None),
            P(everything, None, None),
            P(everything),
            P(("y", "c"), None, None),
            P(("y", "c"), ("x", "z")),
        ),
        out_specs=P(everything, None),
        check_vma=False,
    )
```

```python
import jax
import jax.numpy as jnp
from jax import lax
from jax.experimental import pallas as pl
from jax.experimental.layout import Layout, with_layout_constraint
from jax.experimental.pallas import tpu as pltpu
from jax.sharding import Mesh
from jax.sharding import PartitionSpec as P

score_scale = 192.0 ** (-0.5)
f32 = jnp.float32
bf16 = jnp.bfloat16


def attend_kernel(lengths, queries, cache, latent, near_queries, near_cache, near_latent, arrived, left):
    requests = near_queries.shape[0]
    cores, groups, _, heads, width = near_latent.shape
    pairs = ((queries, near_queries), (cache, near_cache))
    loads = [
        [pltpu.make_async_copy(far.at[r], near.at[r], arrived.at[i, r]) for i, (far, near) in enumerate(pairs)]
        for r in range(requests)
    ]
    for load in loads:
        for copy in load:
            copy.start()
    scores = []
    for r in range(requests):
        for copy in loads[r]:
            copy.wait()
        raw = lax.dot_general(
            near_queries[r], near_cache[r], (((0,), (0,)), ((), ())), preferred_element_type=f32
        )
        scores.append(raw * score_scale)
    stores = []
    for r in range(requests):
        alive = lax.broadcasted_iota(jnp.int32, scores[r].shape, 1) < lengths[r]
        masked = jnp.where(alive, scores[r], -1e30)
        powers = jnp.exp(masked - jnp.max(masked, axis=1, keepdims=True))
        weights = (powers / jnp.sum(powers, axis=1, keepdims=True)).astype(bf16)
        mixture = lax.dot_general(
            weights, near_cache[r, :width], (((1,), (1,)), ((), ())), preferred_element_type=f32
        )
        mixture = mixture.reshape(groups, cores, heads, width).astype(bf16)
        for core in range(cores):
            near_latent[core, :, r] = mixture[:, core]
        stores.append(pltpu.make_async_copy(near_latent.at[:, :, r], latent.at[:, :, r], left.at[r]))
        stores[r].start()
    for store in stores:
        store.wait()


def attend(queries, cache, lengths, groups, cores, width):
    requests, entries, heads = queries.shape
    slots = cache.shape[2]
    shape = (cores, groups, requests, heads // (groups * cores), width)
    anywhere = pl.BlockSpec(memory_space=pl.ANY)
    return pl.pallas_call(
        attend_kernel,
        in_specs=[pl.BlockSpec(memory_space=pltpu.SMEM), anywhere, anywhere],
        out_specs=anywhere,
        out_shape=jax.ShapeDtypeStruct(shape, bf16),
        scratch_shapes=[
            pltpu.VMEM(queries.shape, bf16),
            pltpu.VMEM(cache.shape, bf16),
            pltpu.VMEM(shape, bf16),
            pltpu.SemaphoreType.DMA((2, requests)),
            pltpu.SemaphoreType.DMA((requests,)),
        ],
        cost_estimate=pl.CostEstimate(
            flops=2 * requests * heads * slots * (entries + width),
            transcendentals=requests * heads * slots,
            bytes_accessed=2 * requests * (entries * (heads + slots) + heads * width),
        ),
        name="attend",
    )(lengths, queries, cache)


def local(queries, latent_cache, lengths, value_weight, output_weight):
    nx, nz, ny, nc = (lax.axis_size(a) for a in ("x", "z", "y", "c"))
    x, c = lax.axis_index("x"), lax.axis_index("c")
    requests = queries.shape[0]
    sent = {k: lax.ppermute(output_weight, "x", [(i, (i + k) % nx) for i in range(nx)]) for k in (3, 2, 1)}
    latent = attend(
        queries.transpose(0, 2, 1), latent_cache.transpose(0, 2, 1), lengths, ny, nc, value_weight.shape[1]
    )
    latent = latent.reshape(nc * ny, *latent.shape[2:])
    swapped = lax.all_to_all(latent, ("c", "y"), split_axis=0, concat_axis=0, tiled=True)
    swapped = with_layout_constraint(swapped, Layout(major_to_minor=(0, 1, 2, 3)))
    values = jnp.einsum("trhd,hde->trhe", swapped, value_weight, preferred_element_type=f32)
    values = values.astype(bf16).reshape(nc, ny * requests, -1)

    def gather(values):
        values = jnp.broadcast_to(values[None], (nz, *values.shape))
        return lax.all_to_all(
            values, "z", split_axis=0, concat_axis=0, tiled=True, axis_index_groups=[list(range(nz - 1, -1, -1))]
        )

    everyone = lax.cond(x < nx, gather, lambda v: jnp.zeros((nz, *v.shape), bf16), values)
    everyone, *others = lax.optimization_barrier((everyone, *sent.values()))
    sent = dict(zip(sent, others))
    blocks = [output_weight, *(sent[k] for k in range(1, nx))]

    rows = everyone.transpose(1, 0, 2, 3).reshape(nc * nz * ny * requests, -1)
    both = jnp.concatenate([jnp.dot(rows, w, preferred_element_type=f32) for w in blocks], axis=1)
    first, second = jnp.split(both, nc)
    theirs, mine = jnp.where(c == 0, second, first), jnp.where(c == 0, first, second)
    received = lax.ppermute(theirs, "c", [(i, (i + 1) % nc) for i in range(nc)])
    summed = (mine + received).astype(bf16).reshape(nz * ny, requests, -1)
    summed, turn = lax.optimization_barrier((summed, jnp.mod(nx - x, nx)))
    downward = [[z * ny + y for z in range(nz - 1, -1, -1) for y in range(ny)]]
    parts = lax.all_to_all(
        summed, ("z", "y"), split_axis=0, concat_axis=0, tiled=True, axis_index_groups=downward
    )
    parts = parts.reshape(nz, ny, requests, nx, -1).astype(f32)
    total = parts[:, 0]
    for i in range(1, ny):
        total = total + parts[:, i]
    total = total[::-1].astype(bf16).transpose(1, 2, 0, 3)
    shifted = total[:, :1], total[:, :0:-1]
    total = jnp.concatenate([*shifted, *shifted], axis=1)
    total = lax.dynamic_slice_in_dim(total, turn, nx, 1, allow_negative_indices=False)
    return total.reshape(requests, -1)


def solution(mesh):
    grid = Mesh(mesh.devices.reshape(4, 8, 8, 2), ("x", "z", "y", "c"))
    everything = ("x", "z", "y", "c")
    return jax.shard_map(
        local,
        mesh=grid,
        in_specs=(
            P(everything, None, None),
            P(everything, None, None),
            P(everything),
            P(("y", "c"), None, None),
            P(("y", "c"), ("x", "z")),
        ),
        out_specs=P(everything, None),
        check_vma=False,
    )
```

```python
import jax
import jax.numpy as jnp
from jax import lax
from jax.experimental import pallas as pl
from jax.experimental.layout import Layout, with_layout_constraint
from jax.experimental.pallas import tpu as pltpu
from jax.sharding import Mesh
from jax.sharding import PartitionSpec as P

score_scale = 192.0 ** (-0.5)
f32 = jnp.float32
bf16 = jnp.bfloat16


def attend_kernel(lengths, queries, cache, latent, near_queries, near_cache, near_latent, arrived, left):
    requests = near_queries.shape[0]
    cores, groups, _, heads, width = near_latent.shape
    pairs = ((queries, near_queries), (cache, near_cache))
    loads = [
        [pltpu.make_async_copy(far.at[r], near.at[r], arrived.at[i, r]) for i, (far, near) in enumerate(pairs)]
        for r in range(requests)
    ]
    for load in loads:
        for copy in load:
            copy.start()
    scores = []
    for r in range(requests):
        for copy in loads[r]:
            copy.wait()
        raw = lax.dot_general(
            near_queries[r], near_cache[r], (((0,), (0,)), ((), ())), preferred_element_type=f32
        )
        scores.append(raw * score_scale)
    stores = []
    for r in range(requests):
        alive = lax.broadcasted_iota(jnp.int32, scores[r].shape, 1) < lengths[r]
        masked = jnp.where(alive, scores[r], -1e30)
        powers = jnp.exp(masked - jnp.max(masked, axis=1, keepdims=True))
        weights = (powers / jnp.sum(powers, axis=1, keepdims=True)).astype(bf16)
        mixture = lax.dot_general(
            weights, near_cache[r, :width], (((1,), (1,)), ((), ())), preferred_element_type=f32
        )
        mixture = mixture.reshape(groups, cores, heads, width).astype(bf16)
        for core in range(cores):
            near_latent[core, :, r] = mixture[:, core]
        stores.append(pltpu.make_async_copy(near_latent.at[:, :, r], latent.at[:, :, r], left.at[r]))
        stores[r].start()
    for store in stores:
        store.wait()


def attend(queries, cache, lengths, groups, cores, width):
    requests, entries, heads = queries.shape
    slots = cache.shape[2]
    shape = (cores, groups, requests, heads // (groups * cores), width)
    anywhere = pl.BlockSpec(memory_space=pl.ANY)
    return pl.pallas_call(
        attend_kernel,
        in_specs=[pl.BlockSpec(memory_space=pltpu.SMEM), anywhere, anywhere],
        out_specs=anywhere,
        out_shape=jax.ShapeDtypeStruct(shape, bf16),
        scratch_shapes=[
            pltpu.VMEM(queries.shape, bf16),
            pltpu.VMEM(cache.shape, bf16),
            pltpu.VMEM(shape, bf16),
            pltpu.SemaphoreType.DMA((2, requests)),
            pltpu.SemaphoreType.DMA((requests,)),
        ],
        cost_estimate=pl.CostEstimate(
            flops=2 * requests * heads * slots * (entries + width),
            transcendentals=requests * heads * slots,
            bytes_accessed=2 * requests * (entries * (heads + slots) + heads * width),
        ),
        name="attend",
    )(lengths, queries, cache)


def local(queries, latent_cache, lengths, value_weight, output_weight):
    nx, nz, ny, nc = (lax.axis_size(a) for a in ("x", "z", "y", "c"))
    x, c = lax.axis_index("x"), lax.axis_index("c")
    requests = queries.shape[0]
    sent = {k: lax.ppermute(output_weight, "x", [(i, (i + k) % nx) for i in range(nx)]) for k in (3, 2, 1)}
    latent = attend(
        queries.transpose(0, 2, 1), latent_cache.transpose(0, 2, 1), lengths, ny, nc, value_weight.shape[1]
    )
    latent = latent.reshape(nc * ny, *latent.shape[2:])
    swapped = lax.all_to_all(latent, ("c", "y"), split_axis=0, concat_axis=0, tiled=True)
    swapped = with_layout_constraint(swapped, Layout(major_to_minor=(0, 1, 2, 3)))
    values = jnp.einsum("trhd,hde->trhe", swapped, value_weight, preferred_element_type=f32)
    values = values.astype(bf16).reshape(nc, ny * requests, -1)

    def gather(values):
        values = jnp.broadcast_to(values[None], (nz, *values.shape))
        return lax.all_to_all(
            values, "z", split_axis=0, concat_axis=0, tiled=True, axis_index_groups=[list(range(nz - 1, -1, -1))]
        )

    everyone = lax.cond(x < nx, gather, lambda v: jnp.zeros((nz, *v.shape), bf16), values)
    everyone, *others = lax.optimization_barrier((everyone, *sent.values()))
    sent = dict(zip(sent, others))
    blocks = [output_weight, *(sent[k] for k in range(1, nx))]

    rows = everyone.transpose(1, 0, 2, 3).reshape(nc * nz * ny * requests, -1)
    both = jnp.concatenate([jnp.dot(rows, w, preferred_element_type=f32) for w in blocks], axis=1)
    first, second = jnp.split(both, nc)
    theirs, mine = jnp.where(c == 0, second, first), jnp.where(c == 0, first, second)
    received = lax.ppermute(theirs, "c", [(i, (i + 1) % nc) for i in range(nc)])
    summed = (mine + received).astype(bf16).reshape(nz * ny, requests, -1)
    summed, turn = lax.optimization_barrier((summed, jnp.mod(nx - x, nx)))
    downward = [[z * ny + y for z in range(nz - 1, -1, -1) for y in range(ny)]]
    parts = lax.all_to_all(
        summed, ("z", "y"), split_axis=0, concat_axis=0, tiled=True, axis_index_groups=downward
    )
    parts = parts.reshape(nz, ny, requests, -1).astype(f32)
    total = parts[:, 0]
    for i in range(1, ny):
        total = total + parts[:, i]
    total = lax.optimization_barrier(total.astype(bf16)).reshape(nz, requests, nx, -1)
    total = total[::-1].transpose(1, 2, 0, 3)
    shifted = total[:, :1], total[:, :0:-1]
    total = jnp.concatenate([*shifted, *shifted], axis=1)
    total = lax.dynamic_slice_in_dim(total, turn, nx, 1, allow_negative_indices=False)
    return total.reshape(requests, -1)


def solution(mesh):
    grid = Mesh(mesh.devices.reshape(4, 8, 8, 2), ("x", "z", "y", "c"))
    everything = ("x", "z", "y", "c")
    return jax.shard_map(
        local,
        mesh=grid,
        in_specs=(
            P(everything, None, None),
            P(everything, None, None),
            P(everything),
            P(("y", "c"), None, None),
            P(("y", "c"), ("x", "z")),
        ),
        out_specs=P(everything, None),
        check_vma=False,
    )
```

```python
import jax
import jax.numpy as jnp
from jax import lax
from jax.experimental import pallas as pl
from jax.experimental.layout import Layout, with_layout_constraint
from jax.experimental.pallas import tpu as pltpu
from jax.sharding import Mesh
from jax.sharding import PartitionSpec as P

score_scale = 192.0 ** (-0.5)
f32 = jnp.float32
bf16 = jnp.bfloat16


def attend_kernel(lengths, queries, cache, latent, near_queries, near_cache, near_latent, arrived, left):
    requests = near_queries.shape[0]
    cores, groups, _, heads, width = near_latent.shape
    pairs = ((queries, near_queries), (cache, near_cache))
    loads = [
        [pltpu.make_async_copy(far.at[r], near.at[r], arrived.at[i, r]) for i, (far, near) in enumerate(pairs)]
        for r in range(requests)
    ]
    for load in loads:
        for copy in load:
            copy.start()
    scores = []
    for r in range(requests):
        for copy in loads[r]:
            copy.wait()
        raw = lax.dot_general(
            near_queries[r], near_cache[r], (((0,), (0,)), ((), ())), preferred_element_type=f32
        )
        scores.append(raw * score_scale)
    stores = []
    for r in range(requests):
        alive = lax.broadcasted_iota(jnp.int32, scores[r].shape, 1) < lengths[r]
        masked = jnp.where(alive, scores[r], -1e30)
        powers = jnp.exp(masked - jnp.max(masked, axis=1, keepdims=True))
        weights = (powers / jnp.sum(powers, axis=1, keepdims=True)).astype(bf16)
        mixture = lax.dot_general(
            weights, near_cache[r, :width], (((1,), (1,)), ((), ())), preferred_element_type=f32
        )
        mixture = mixture.reshape(groups, cores, heads, width).astype(bf16)
        for core in range(cores):
            near_latent[core, :, r] = mixture[:, core]
        stores.append(pltpu.make_async_copy(near_latent.at[:, :, r], latent.at[:, :, r], left.at[r]))
        stores[r].start()
    for store in stores:
        store.wait()


def attend(queries, cache, lengths, groups, cores, width):
    requests, entries, heads = queries.shape
    slots = cache.shape[2]
    shape = (cores, groups, requests, heads // (groups * cores), width)
    anywhere = pl.BlockSpec(memory_space=pl.ANY)
    return pl.pallas_call(
        attend_kernel,
        in_specs=[pl.BlockSpec(memory_space=pltpu.SMEM), anywhere, anywhere],
        out_specs=anywhere,
        out_shape=jax.ShapeDtypeStruct(shape, bf16),
        scratch_shapes=[
            pltpu.VMEM(queries.shape, bf16),
            pltpu.VMEM(cache.shape, bf16),
            pltpu.VMEM(shape, bf16),
            pltpu.SemaphoreType.DMA((2, requests)),
            pltpu.SemaphoreType.DMA((requests,)),
        ],
        cost_estimate=pl.CostEstimate(
            flops=2 * requests * heads * slots * (entries + width),
            transcendentals=requests * heads * slots,
            bytes_accessed=2 * requests * (entries * (heads + slots) + heads * width),
        ),
        name="attend",
    )(lengths, queries, cache)


def local(queries, latent_cache, lengths, value_weight, output_weight):
    nx, nz, ny, nc = (lax.axis_size(a) for a in ("x", "z", "y", "c"))
    x, c = lax.axis_index("x"), lax.axis_index("c")
    requests = queries.shape[0]
    sent = {k: lax.ppermute(output_weight, "x", [(i, (i + k) % nx) for i in range(nx)]) for k in (3, 2, 1)}
    latent = attend(
        queries.transpose(0, 2, 1), latent_cache.transpose(0, 2, 1), lengths, ny, nc, value_weight.shape[1]
    )
    latent = latent.reshape(nc * ny, *latent.shape[2:])
    swapped = lax.all_to_all(latent, ("c", "y"), split_axis=0, concat_axis=0, tiled=True)
    swapped = with_layout_constraint(swapped, Layout(major_to_minor=(0, 1, 2, 3)))
    values = jnp.einsum("trhd,hde->trhe", swapped, value_weight, preferred_element_type=f32)
    values = values.astype(bf16).reshape(nc, ny * requests, -1)

    def gather(values):
        values = jnp.broadcast_to(values[None], (nz, *values.shape))
        return lax.all_to_all(
            values, "z", split_axis=0, concat_axis=0, tiled=True, axis_index_groups=[list(range(nz - 1, -1, -1))]
        )

    everyone = lax.cond(x < nx, gather, lambda v: jnp.zeros((nz, *v.shape), bf16), values)
    everyone, *others = lax.optimization_barrier((everyone, *sent.values()))
    sent = dict(zip(sent, others))
    blocks = [output_weight, *(sent[k] for k in range(1, nx))]

    rows = everyone.transpose(1, 0, 2, 3).reshape(nc * nz * ny * requests, -1)
    both = jnp.concatenate([jnp.dot(rows, w, preferred_element_type=f32) for w in blocks], axis=1)
    first, second = jnp.split(both, nc)
    theirs, mine = jnp.where(c == 0, second, first), jnp.where(c == 0, first, second)
    received = lax.ppermute(theirs.astype(bf16), "c", [(i, (i + 1) % nc) for i in range(nc)])
    summed = (mine + received).astype(bf16).reshape(nz * ny, requests, -1)
    summed, turn = lax.optimization_barrier((summed, jnp.mod(nx - x, nx)))
    downward = [[z * ny + y for z in range(nz - 1, -1, -1) for y in range(ny)]]
    parts = lax.all_to_all(
        summed, ("z", "y"), split_axis=0, concat_axis=0, tiled=True, axis_index_groups=downward
    )
    parts = parts.reshape(nz, ny, requests, -1).astype(f32)
    total = parts[:, 0]
    for i in range(1, ny):
        total = total + parts[:, i]
    total = lax.optimization_barrier(total.astype(bf16)).reshape(nz, requests, nx, -1)
    total = total[::-1].transpose(1, 2, 0, 3)
    shifted = total[:, :1], total[:, :0:-1]
    total = jnp.concatenate([*shifted, *shifted], axis=1)
    total = lax.dynamic_slice_in_dim(total, turn, nx, 1, allow_negative_indices=False)
    return total.reshape(requests, -1)


def solution(mesh):
    grid = Mesh(mesh.devices.reshape(4, 8, 8, 2), ("x", "z", "y", "c"))
    everything = ("x", "z", "y", "c")
    return jax.shard_map(
        local,
        mesh=grid,
        in_specs=(
            P(everything, None, None),
            P(everything, None, None),
            P(everything),
            P(("y", "c"), None, None),
            P(("y", "c"), ("x", "z")),
        ),
        out_specs=P(everything, None),
        check_vma=False,
    )
```

```python
import jax
import jax.numpy as jnp
from jax import lax
from jax.experimental import pallas as pl
from jax.experimental.layout import Layout, with_layout_constraint
from jax.experimental.pallas import tpu as pltpu
from jax.sharding import Mesh
from jax.sharding import PartitionSpec as P

score_scale = 192.0 ** (-0.5)
f32 = jnp.float32
bf16 = jnp.bfloat16


def attend_kernel(lengths, queries, cache, latent, near_queries, near_cache, near_latent, arrived, left):
    requests = near_queries.shape[0]
    cores, groups, _, heads, width = near_latent.shape
    pairs = ((queries, near_queries), (cache, near_cache))
    loads = [
        [pltpu.make_async_copy(far.at[r], near.at[r], arrived.at[i, r]) for i, (far, near) in enumerate(pairs)]
        for r in range(requests)
    ]
    for load in loads:
        for copy in load:
            copy.start()
    scores = []
    for r in range(requests):
        for copy in loads[r]:
            copy.wait()
        raw = lax.dot_general(
            near_queries[r], near_cache[r], (((0,), (0,)), ((), ())), preferred_element_type=f32
        )
        scores.append(raw * score_scale)
    stores = []
    for r in range(requests):
        alive = lax.broadcasted_iota(jnp.int32, scores[r].shape, 1) < lengths[r]
        masked = jnp.where(alive, scores[r], -1e30)
        powers = jnp.exp(masked - jnp.max(masked, axis=1, keepdims=True))
        weights = (powers / jnp.sum(powers, axis=1, keepdims=True)).astype(bf16)
        mixture = lax.dot_general(
            weights, near_cache[r, :width], (((1,), (1,)), ((), ())), preferred_element_type=f32
        )
        mixture = mixture.reshape(groups, cores, heads, width).astype(bf16)
        for core in range(cores):
            near_latent[core, :, r] = mixture[:, core]
        stores.append(pltpu.make_async_copy(near_latent.at[:, :, r], latent.at[:, :, r], left.at[r]))
        stores[r].start()
    for store in stores:
        store.wait()


def attend(queries, cache, lengths, groups, cores, width):
    requests, entries, heads = queries.shape
    slots = cache.shape[2]
    shape = (cores, groups, requests, heads // (groups * cores), width)
    anywhere = pl.BlockSpec(memory_space=pl.ANY)
    return pl.pallas_call(
        attend_kernel,
        in_specs=[pl.BlockSpec(memory_space=pltpu.SMEM), anywhere, anywhere],
        out_specs=anywhere,
        out_shape=jax.ShapeDtypeStruct(shape, bf16),
        scratch_shapes=[
            pltpu.VMEM(queries.shape, bf16),
            pltpu.VMEM(cache.shape, bf16),
            pltpu.VMEM(shape, bf16),
            pltpu.SemaphoreType.DMA((2, requests)),
            pltpu.SemaphoreType.DMA((requests,)),
        ],
        cost_estimate=pl.CostEstimate(
            flops=2 * requests * heads * slots * (entries + width),
            transcendentals=requests * heads * slots,
            bytes_accessed=2 * requests * (entries * (heads + slots) + heads * width),
        ),
        name="attend",
    )(lengths, queries, cache)


def local(queries, latent_cache, lengths, value_weight, output_weight):
    nx, nz, ny, nc = (lax.axis_size(a) for a in ("x", "z", "y", "c"))
    x, c = lax.axis_index("x"), lax.axis_index("c")
    requests = queries.shape[0]
    sent = {k: lax.ppermute(output_weight, "x", [(i, (i + k) % nx) for i in range(nx)]) for k in (3, 2, 1)}
    latent = attend(
        queries.transpose(0, 2, 1), latent_cache.transpose(0, 2, 1), lengths, ny, nc, value_weight.shape[1]
    )
    latent = latent.reshape(nc * ny, *latent.shape[2:])
    swapped = lax.all_to_all(latent, ("c", "y"), split_axis=0, concat_axis=0, tiled=True)
    swapped = with_layout_constraint(swapped, Layout(major_to_minor=(0, 1, 2, 3)))
    values = jnp.einsum("trhd,hde->trhe", swapped, value_weight, preferred_element_type=f32)
    values = values.astype(bf16).reshape(nc, ny * requests, -1)

    def gather(values):
        values = jnp.broadcast_to(values[None], (nz, *values.shape))
        return lax.all_to_all(
            values, "z", split_axis=0, concat_axis=0, tiled=True, axis_index_groups=[list(range(nz - 1, -1, -1))]
        )

    everyone = lax.cond(x < nx, gather, lambda v: jnp.zeros((nz, *v.shape), bf16), values)
    everyone, *others = lax.optimization_barrier((everyone, *sent.values()))
    sent = dict(zip(sent, others))
    blocks = [output_weight, *(sent[k] for k in range(nx - 1, 0, -1))]

    rows = everyone.transpose(1, 0, 2, 3).reshape(nc * nz * ny * requests, -1)
    both = jnp.concatenate([jnp.dot(rows, w, preferred_element_type=f32) for w in blocks], axis=1)
    first, second = jnp.split(both, nc)
    theirs, mine = jnp.where(c == 0, second, first), jnp.where(c == 0, first, second)
    received = lax.ppermute(theirs.astype(bf16), "c", [(i, (i + 1) % nc) for i in range(nc)])
    summed = (mine + received).astype(bf16).reshape(nz * ny, requests, -1)
    summed, turn = lax.optimization_barrier((summed, jnp.mod(nx - x, nx)))
    downward = [[z * ny + y for z in range(nz - 1, -1, -1) for y in range(ny)]]
    parts = lax.all_to_all(
        summed, ("z", "y"), split_axis=0, concat_axis=0, tiled=True, axis_index_groups=downward
    )
    parts = parts.reshape(nz, ny, requests, -1).astype(f32)
    total = parts[:, 0]
    for i in range(1, ny):
        total = total + parts[:, i]
    total = lax.optimization_barrier(total.astype(bf16)).reshape(nz, requests, nx, -1)
    total = total[::-1].transpose(1, 2, 0, 3)
    total = jnp.concatenate([total, total], axis=1)
    total = lax.dynamic_slice_in_dim(total, turn, nx, 1, allow_negative_indices=False)
    return total.reshape(requests, -1)


def solution(mesh):
    grid = Mesh(mesh.devices.reshape(4, 8, 8, 2), ("x", "z", "y", "c"))
    everything = ("x", "z", "y", "c")
    return jax.shard_map(
        local,
        mesh=grid,
        in_specs=(
            P(everything, None, None),
            P(everything, None, None),
            P(everything),
            P(("y", "c"), None, None),
            P(("y", "c"), ("x", "z")),
        ),
        out_specs=P(everything, None),
        check_vma=False,
    )
```
